256 devices in a mesh: seq: 32 (over z, x_hi, core), tp: 8 (over x_lo, y).
Axes of the slice: x: 4 (x_hi: 2, x_lo: 2; x = x_hi * 2 + x_lo), y: 4, z: 8, core: 2. Of those that a mesh axis runs over, the one named last changes fastest.
Arguments:
- query: bfloat16 [8192, 3584], P('seq', 'tp'), may hold values from -6 to 6
- keys: bfloat16 [8192, 3584], P('seq', 'tp'), may hold values from -6 to 6
- values: bfloat16 [8192, 3584], P('seq', 'tp'), may hold values from -6 to 6
- prefix_keys: bfloat16 [4096, 3584], P('seq', 'tp'), may hold values from -6 to 6
- prefix_values: bfloat16 [4096, 3584], P('seq', 'tp'), may hold values from -6 to 6
- residual: bfloat16 [8192, 3584], P('seq', 'tp'), may hold values from -4 to 4
- out_weight: bfloat16 [3584, 3584], P('tp'), may hold values from -1 to 1
- suffix_lens: int32 [16], replicated, may hold values from 1 to 2048, 8192 in all
- req_group: int32 [16], replicated, may hold values from 0 to 3
- placement: int32 [8192], replicated, may hold values from 0 to 8191, each once
- prefix_owner: int32 [32], replicated, may hold values from 0 to 3, as said below
Outputs:
- hidden: bfloat16 [8192, 3584], P('seq', 'tp')
- cache_keys: bfloat16 [8192, 3584], P('seq', 'tp')
- cache_values: bfloat16 [8192, 3584], P('seq', 'tp')
The draws below stay inside these ranges and needn't reach their ends.
Inputs may be any that keep to these rules, and one draw needn't show every extreme that they name: `prefix_owner`: each group number appears exactly 8 times.
All inputs are finite; a program needn't handle non-finite values.
Results may differ from the reference program's by a relative error of at most 0.014.
Values may be sent and summed in bfloat16 or wider, within the bound.
A program may use at most 128 MiB of HBM per device.

```python
import math
import jax
import jax.numpy as jnp
import numpy as np
from jax import lax

D = 3584
HEADS = 16
HD = 224
TOK_DEV = 256
PREF = 1024
GROUPS = 4
REQS = 16
TOKENS = 8192
HC = 3584
OWNERS = 8
PBLK = 128
N_SEQ = 32


def draw_prefix_owner(key, part):
    order = jax.random.permutation(jax.random.fold_in(key, 7), OWNERS * GROUPS)
    return (order % GROUPS).astype(jnp.int32)


def sign_pattern(key):
    bits = jax.random.bernoulli(jax.random.fold_in(key, 101), 0.5, (HEADS, HD))
    return jnp.where(bits, 1.0, -1.0).astype(jnp.float32).reshape(HEADS * HD)


def head_strengths(table):
    level = jnp.arange(HEADS * HD, dtype=jnp.int32) // HD % 4
    result = jnp.zeros((HEADS * HD,), jnp.float32)
    for slot in range(4):
        result = jnp.where(level == slot, table[slot], result)
    return result


def chosen_suffix(key):
    return jax.random.randint(jax.random.fold_in(key, 102), (TOKENS,), 0, 32) == 0


def chosen_prefix(key):
    offsets = jax.random.randint(jax.random.fold_in(key, 103), (OWNERS * GROUPS,), 0, PBLK)
    within = jnp.arange(GROUPS * PREF, dtype=jnp.int32) % PBLK
    return within == jnp.repeat(offsets, PBLK)


def draw_query(key, part):
    inner = jax.random.fold_in(key, 1)
    base = jnp.clip(jax.random.normal(inner, (TOKENS, HEADS * HD), jnp.float32), -5.5, 5.5)
    planted = sign_pattern(key) * head_strengths((2.75, 3.5, 4.25, 5.0))
    return jnp.where(chosen_suffix(key)[:, None], planted[None, :], base).astype(jnp.bfloat16)


def draw_keys(key, part):
    inner = jax.random.fold_in(key, 2)
    base = jnp.clip(jax.random.normal(inner, (TOKENS, HEADS * HD), jnp.float32), -5.5, 5.5)
    planted = sign_pattern(key) * head_strengths((2.75, 3.5, 4.25, 5.0))
    return jnp.where(chosen_suffix(key)[:, None], planted[None, :], base).astype(jnp.bfloat16)


def draw_prefix_keys(key, part):
    inner = jax.random.fold_in(key, 3)
    base = jnp.clip(jax.random.normal(inner, (GROUPS * PREF, HEADS * HD), jnp.float32), -5.5, 5.5)
    planted = sign_pattern(key) * head_strengths((2.703125, 3.46875, 4.21875, 4.96875))
    return jnp.where(chosen_prefix(key)[:, None], planted[None, :], base).astype(jnp.bfloat16)


def set_ends(entries, stream_key, low, largest):
    place = [jax.random.randint(jax.random.fold_in(stream_key, axis), (), 0, length) for axis, length in enumerate(entries.shape)]
    widest = entries.shape.index(max(entries.shape))
    beside = place[:widest] + [(place[widest] + 1) % entries.shape[widest]] + place[widest + 1:]
    return entries.at[tuple(place)].set(low).at[tuple(beside)].set(largest)


def level_of(rng, shape, split, low, top_value):
    def one(dim, blocks):
        draws = jax.random.uniform(jax.random.fold_in(jax.random.fold_in(rng, 6), dim), (blocks,), jnp.float32, low / len(split), top_value / len(split))
        return jnp.repeat(jnp.exp(draws), shape[dim] // blocks).reshape((-1,) + (1,) * (len(shape) - dim - 1))

    loudness = one(*split[0])
    for cut in split[1:]:
        loudness = loudness * one(*cut)
    return loudness


def profile(number_of, total, reach, lean):
    loads = [(1 << 20) // math.isqrt(standing ** lean) + 1 for standing in range(2, number_of + 1)]
    spare, counts = total - reach - (number_of - 1), [1] * (number_of - 1)
    while spare > 0:
        movable = [i for i in range(number_of - 1) if counts[i] < reach]
        whole, left = sum([loads[i] for i in movable]), spare
        for i in movable:
            addition = min(reach - counts[i], max(1, left * loads[i] // whole), spare)
            counts[i] = counts[i] + addition
            spare = spare - addition
    return np.array([reach] + counts)


def ragged_sizes(own_key, count, total, bound, skew):
    if count == 2:
        one = jax.random.randint(own_key, (), max(1, total - bound), min(bound, total - 1) + 1)
        return jnp.stack([one, total - one])
    lengths = jnp.asarray(profile(count, total, bound, skew), jnp.int32)
    twos = (count - 1) // 2
    giver, taker = lengths[1:1 + 2 * twos:2], lengths[2:2 + 2 * twos:2]
    room = jnp.minimum(giver - 1, bound - taker)
    passed = jax.random.randint(jax.random.fold_in(own_key, 1), (twos,), 0, 1 << 20) % (room + 1)
    lengths = lengths.at[1:1 + 2 * twos:2].set(giver - passed).at[2:2 + 2 * twos:2].set(taker + passed)
    return lengths[jax.random.permutation(jax.random.fold_in(own_key, 2), count)]


def gaussian(rng, dims, spread, limit, cuts=(), kind=jnp.bfloat16):
    values = jax.random.normal(rng, dims, jnp.float32) * spread
    if len(cuts) > 0:
        values = level_of(rng, dims, cuts, -0.22, 0.18) * values
    return jnp.clip(values, min=-limit, max=limit).astype(kind)


def setup_inputs(seed: int = 0) -> dict:
    streams_of = jax.random.split(jax.random.key(seed), 12)
    query = draw_query(jax.random.fold_in(streams_of[11], 71), 0)
    keys = draw_keys(jax.random.fold_in(streams_of[11], 71), 0)
    values = gaussian(streams_of[2], (TOKENS, HC), 1.0, 6.0, ((0, 32), (1, 8)))
    prefix_keys = draw_prefix_keys(jax.random.fold_in(streams_of[11], 71), 0)
    prefix_values = gaussian(streams_of[4], (GROUPS * PREF, HC), 1.0, 6.0, ((0, 32), (1, 8)))
    residual = gaussian(streams_of[5], (TOKENS, D), 0.3, 4.0, ((0, 32), (1, 8)))
    out_weight = gaussian(streams_of[6], (HC, D), (4.0 / (HEADS * HD) ** 0.5), 1.0, ((0, 8),))
    suffix_lens = ragged_sizes(streams_of[7], REQS, TOKENS, TOKENS // 4, 2).astype(jnp.int32)
    req_group = set_ends(jax.random.randint(streams_of[8], (REQS,), 0, GROUPS), jax.random.fold_in(streams_of[8], 1), 0, GROUPS - 1).astype(jnp.int32)
    placement = jax.random.permutation(streams_of[9], TOKENS).astype(jnp.int32)
    prefix_owner = draw_prefix_owner(jax.random.fold_in(streams_of[11], 71), 0)
    return {"query": query, "keys": keys, "values": values, "prefix_keys": prefix_keys, "prefix_values": prefix_values, "residual": residual, "out_weight": out_weight, "suffix_lens": suffix_lens, "req_group": req_group, "placement": placement, "prefix_owner": prefix_owner}


def reference(query, keys, values, prefix_keys, prefix_values, residual, out_weight, suffix_lens, req_group, placement, prefix_owner):
    ends = jnp.cumsum(suffix_lens).astype(jnp.int32)
    req = lax.optimization_barrier(jnp.sum((placement[:, None] >= ends[None, :]).astype(jnp.int32), axis=1))
    grp = req_group[req]
    pgrp = jnp.repeat(prefix_owner, PBLK)
    key_all = jnp.concatenate([keys, prefix_keys], axis=0).reshape(-1, HEADS, HD).astype(jnp.float32)
    value_all = jnp.concatenate([values, prefix_values], axis=0).reshape(-1, HEADS, HD).astype(jnp.float32)
    scale = 1.0 / math.sqrt(HD)

    def one_block(index):
        first = (index * TOK_DEV).astype(jnp.int32)
        queries = lax.dynamic_slice_in_dim(query, first, TOK_DEV).reshape(TOK_DEV, HEADS, HD).astype(jnp.float32)
        block_pos = lax.dynamic_slice_in_dim(placement, first, TOK_DEV)
        block_req = lax.dynamic_slice_in_dim(req, first, TOK_DEV)
        block_grp = lax.dynamic_slice_in_dim(grp, first, TOK_DEV)
        suffix_seen = (req[None, :] == block_req[:, None]) & (placement[None, :] <= block_pos[:, None])
        prefix_seen = pgrp[None, :] == block_grp[:, None]
        visible = jnp.concatenate([suffix_seen, prefix_seen], axis=1)
        scores = jnp.einsum('qhd,khd->hqk', queries, key_all) * scale
        scores = jnp.where(visible[None], scores, -1e+30)
        top = lax.optimization_barrier(jnp.max(scores, axis=2, keepdims=True))
        weights = jnp.where(visible[None], jnp.exp(scores - top), 0.0).astype(jnp.bfloat16).astype(jnp.float32)
        total = lax.optimization_barrier(jnp.sum(weights, axis=2))
        summed = jnp.einsum('hqk,khd->hqd', weights, value_all)
        attended = summed / total[:, :, None]
        return jnp.transpose(attended, (1, 0, 2)).reshape(TOK_DEV, HC).astype(jnp.bfloat16)
    attended = lax.map(one_block, jnp.arange(N_SEQ, dtype=jnp.int32)).reshape(TOKENS, HC)
    projected = jnp.dot(attended, out_weight, preferred_element_type=jnp.float32)
    hidden = (residual.astype(jnp.float32) + projected).astype(jnp.bfloat16)
    cache_keys = jnp.zeros_like(keys).at[placement].set(keys)
    cache_values = jnp.zeros_like(values).at[placement].set(values)
    return (hidden, cache_keys, cache_values)
```

```python
import math

import jax
import jax.numpy as jnp
from jax import lax
from jax.experimental import pallas as pl
from jax.experimental.pallas import tpu as pltpu
from jax.sharding import PartitionSpec as P

HD = 224
ROWS = 256
PBLK = 128
PART = ROWS + PBLK
LANES = 2 * PART
QN = 2 * ROWS
KV = 2 * HD
AUG = KV + 16
NZ = 8
TQ = 256
NEG = -1e30
COEF = math.log2(math.e) / math.sqrt(HD)
MESH = pl.DeviceIdType.MESH
NT = (((1,), (1,)), ((), ()))


def attention_kernel(
    lens_ref,
    group_ref,
    owner_ref,
    pos_ref,
    q_ref,
    k_ref,
    v_ref,
    pk_ref,
    pv_ref,
    att_ref,
    ck_ref,
    cv_ref,
    gathered,
    q_other,
    q_rows,
    q_pos,
    q_start,
    q_grp,
    top,
    accum,
    cache,
    att_send,
    cache_send,
    att_recv,
    cache_recv,
    ring_send,
    ring_recv,
    twin_send,
    twin_recv,
    pair_send,
    pair_recv,
):
    seq = lax.axis_index("seq")
    tp = lax.axis_index("tp")
    z = seq // 4
    xh = (seq // 2) % 2
    core = seq % 2
    other = 1 - xh
    twin = 1 - core

    def dev(zz, xx, cc):
        return (zz * 4 + xx * 2 + cc, tp)

    up = dev(lax.rem(z + 1, NZ), xh, core)
    down = dev(lax.rem(z + NZ - 1, NZ), xh, core)
    pair = dev(z, other, core)
    sibling = dev(z, xh, twin)

    barrier = pltpu.get_barrier_semaphore()
    for peer in (up, down, pair, sibling):
        pl.semaphore_signal(barrier, inc=1, device_id=peer, device_id_type=MESH)
    pl.semaphore_wait(barrier, 4)

    mine = pl.multiple_of(xh * HD, 32)
    theirs = pl.multiple_of(other * HD, 32)
    mine_lane = pl.multiple_of(xh * PART, 128)
    theirs_lane = pl.multiple_of(other * PART, 128)

    def remote(src, dst, send, recv, device):
        return pltpu.make_async_remote_copy(
            src_ref=src,
            dst_ref=dst,
            send_sem=send,
            recv_sem=recv,
            device_id=device,
            device_id_type=MESH,
        )

    home = gathered.at[z, core]

    def pair_copies():
        pairs = (
            (k_ref, 0, 0, ROWS),
            (pk_ref, 0, ROWS, PBLK),
            (v_ref, HD, 0, ROWS),
            (pv_ref, HD, ROWS, PBLK),
        )
        copies = [
            remote(
                ref.at[pl.ds(theirs, HD)],
                home.at[pl.ds(row, HD), pl.ds(pl.multiple_of(mine_lane + lane, 128), width)],
                pair_send.at[i],
                pair_recv.at[i],
                pair,
            )
            for i, (ref, row, lane, width) in enumerate(pairs)
        ]
        copies.append(
            remote(q_ref.at[pl.ds(theirs, HD)], q_other, pair_send.at[4], pair_recv.at[4], pair)
        )
        return copies

    exchange = pair_copies()
    for copy in exchange:
        copy.start()

    for ref, row, lane, width in (
        (k_ref, 0, 0, ROWS),
        (pk_ref, 0, ROWS, PBLK),
        (v_ref, HD, 0, ROWS),
        (pv_ref, HD, ROWS, PBLK),
    ):
        gathered[z, core, pl.ds(row, HD), pl.ds(pl.multiple_of(mine_lane + lane, 128), width)] = (
            ref[pl.ds(mine, HD), :]
        )

    def quarter(slot, part, kv):
        lane = pl.multiple_of(part * PART, 128)
        row = pl.multiple_of(kv * HD, 32)
        return gathered.at[slot, core, pl.ds(row, HD), pl.ds(lane, PART)]

    def ring(direction, slot, part, kv, index, device):
        ref = quarter(slot, part, kv)
        return remote(
            ref, ref, ring_send.at[direction, index], ring_recv.at[direction, index], device
        )

    def twin_copy(slot, part):
        lane = pl.multiple_of(part * PART, 128)
        ref = gathered.at[slot, core, pl.ds(0, KV), pl.ds(lane, PART)]
        index = slot * 2 + part
        return remote(ref, ref, twin_send.at[index], twin_recv.at[index], sibling)

    def twin_arrival(slot, part):
        lane = pl.multiple_of(part * PART, 128)
        ref = gathered.at[slot, twin, pl.ds(0, KV), pl.ds(lane, PART)]
        index = slot * 2 + part
        return remote(ref, ref, twin_send.at[index], twin_recv.at[index], sibling)

    for kv in range(2):
        ring(0, z, xh, kv, 4 + kv, up).start()
        ring(1, z, xh, kv, 4 + kv, down).start()
    twin_copy(z, xh).start()

    ones = jnp.ones((16, LANES), jnp.bfloat16)
    for slot in range(NZ):
        for cc in range(2):
            gathered[slot, cc, pl.ds(KV, 16), :] = ones

    wide = (ROWS, 128)
    lane_ids = lax.broadcasted_iota(jnp.int32, (128, 128), 1)
    row_ids = lax.broadcasted_iota(jnp.int32, (128, 128), 0)
    for half in range(2):
        source = z * 4 + half * 2 + core
        for piece in range(2):
            row = pos_ref[pl.ds(source * 2 + piece, 1), :]
            spread = jnp.where(lane_ids == row_ids, jnp.broadcast_to(row, (128, 128)), 0)
            column = jnp.sum(spread.astype(jnp.float32), axis=1, keepdims=True)
            column = jnp.broadcast_to(column.astype(jnp.int32), (128, 128))
            q_pos[pl.ds(half * ROWS + piece * 128, 128), :] = column
    position = q_pos[...]
    start = jnp.zeros_like(position)
    group = jnp.full_like(position, group_ref[0])
    end = jnp.int32(0)
    for r in range(15):
        end = end + lens_ref[r]
        past = position >= end
        start = jnp.where(past, end, start)
        group = jnp.where(past, group_ref[r + 1], group)
    q_start[...] = start
    q_grp[...] = group
    top[...] = jnp.full_like(top, NEG)
    accum[...] = jnp.zeros_like(accum)
    cache[...] = jnp.zeros_like(cache)
    own_q = pl.multiple_of(xh * ROWS, ROWS)
    other_q = pl.multiple_of(other * ROWS, ROWS)
    q_rows[pl.ds(own_q, ROWS), :] = jnp.transpose(
        q_ref[pl.ds(mine, HD), :].astype(jnp.float32)
    ).astype(jnp.bfloat16)

    for copy in exchange[:4]:
        copy.wait_recv()
    for kv in range(2):
        ring(0, z, other, kv, 6 + kv, up).start()
        ring(1, z, other, kv, 6 + kv, down).start()
    twin_copy(z, other).start()
    exchange[4].wait_recv()
    q_rows[pl.ds(other_q, ROWS), :] = jnp.transpose(q_other[...].astype(jnp.float32)).astype(
        jnp.bfloat16
    )

    packed = lax.broadcasted_iota(jnp.int32, (ROWS, 128), 0) + (z * 4 + core) * ROWS

    def unit(slot, cc):
        def tile(step, carry):
            rows = pl.ds(pl.multiple_of(step * TQ, TQ), TQ)
            queries = q_rows[rows, :]
            scores = jnp.dot(
                queries, gathered[slot, cc, pl.ds(0, HD), :], preferred_element_type=jnp.float32
            )
            position = q_pos[rows, :]
            start = q_start[rows, :]
            group = q_grp[rows, :]
            pieces = []
            for part in range(2):
                source = slot * 4 + part * 2 + cc
                for piece in range(2):
                    at = part * PART + piece * 128
                    keys = pos_ref[pl.ds(source * 2 + piece, 1), :]
                    seen = (keys <= position) & (keys >= start)
                    pieces.append(jnp.where(seen, scores[:, at : at + 128], NEG))
                at = part * PART + ROWS
                pieces.append(
                    jnp.where(group == owner_ref[source], scores[:, at : at + 128], NEG)
                )
            scores = jnp.concatenate(pieces, axis=1)
            before = top[rows, :]
            fresh = jnp.maximum(before, jnp.max(scores, axis=1, keepdims=True))
            weights = jnp.exp2((scores - jnp.tile(fresh, (1, LANES // 128))) * COEF)
            factor = jnp.exp2((before - fresh) * COEF)
            top[rows, :] = fresh
            added = lax.dot_general(
                weights.astype(jnp.bfloat16),
                gathered[slot, cc, pl.ds(HD, HD + 16), :],
                NT,
                preferred_element_type=jnp.float32,
            )
            accum[rows, :] = accum[rows, :] * factor[:, :1] + added
            return carry

        lax.fori_loop(0, QN // TQ, tile, 0)

        for half in range(2):
            for part in range(2):
                source = slot * 4 + part * 2 + cc
                hot = [
                    jnp.where(
                        pos_ref[pl.ds(source * 2 + piece, 1), :] == packed + half * 2 * ROWS,
                        1.0,
                        0.0,
                    ).astype(jnp.bfloat16)
                    for piece in range(2)
                ]
                cache[half] += lax.dot_general(
                    gathered[slot, cc, pl.ds(0, KV), pl.ds(part * PART, ROWS)],
                    jnp.concatenate(hot, axis=1),
                    NT,
                    preferred_element_type=jnp.float32,
                )

    def slot_of(k, direction):
        return lax.rem(z + jnp.where(direction == 0, NZ - k, k), NZ)

    def step(t, carry):
        k = t // 4 + 1
        i = t % 4
        below = lax.rem(z + NZ - k, NZ)
        above = lax.rem(z + k, NZ)
        first = i < 2
        part = jnp.where(first, xh, other)
        kv = i % 2
        index = k * 4 + i

        @pl.when(k < 4)
        def _():
            ring(0, below, part, kv, index, up).wait_recv()

            @pl.when((k < 3) | first)
            def _():
                ring(0, below, part, kv, index + 4, up).start()

            ring(1, above, part, kv, index, down).wait_recv()

            @pl.when(k < 3)
            def _():
                ring(1, above, part, kv, index + 4, down).start()

            @pl.when((k == 3) & (i >= 2))
            def _():
                ring(1, above, part, kv, index + 2, down).start()

            @pl.when(kv == 1)
            def _():
                twin_copy(below, part).start()
                twin_copy(above, part).start()

        @pl.when((k == 4) & first)
        def _():
            ring(0, below, xh, kv, index, up).wait_recv()
            ring(1, above, other, kv, index, down).wait_recv()

            @pl.when(kv == 1)
            def _():
                twin_copy(below, xh).start()
                twin_copy(below, other).start()

        @pl.when((k > 1) | first)
        def _():
            direction = i // 2
            from_twin = i % 2
            slot = slot_of(k - 1, direction)

            @pl.when(from_twin == 1)
            def _():
                twin_arrival(slot, 0).wait_recv()
                twin_arrival(slot, 1).wait_recv()

            unit(slot, jnp.where(from_twin == 1, twin, core))

        return carry

    lax.fori_loop(0, 16, step, 0)

    def last(from_twin, carry):
        slot = lax.rem(z + 4, NZ)

        @pl.when(from_twin == 1)
        def _():
            twin_arrival(slot, 0).wait_recv()
            twin_arrival(slot, 1).wait_recv()

        unit(slot, jnp.where(from_twin == 1, twin, core))
        return carry

    lax.fori_loop(0, 2, last, 0)

    def finished(at):
        block = accum[pl.ds(at, ROWS), :]
        scaled = block[:, :HD] / block[:, HD : HD + 1]
        return jnp.transpose(scaled).astype(jnp.bfloat16)

    att_send[...] = finished(other_q)
    result = [remote(att_send, att_recv, pair_send.at[5], pair_recv.at[5], pair)]
    result[0].start()
    for i in range(2):
        cache_send[i] = cache[other, pl.ds(i * HD, HD), :].astype(jnp.bfloat16)
        copy = remote(
            cache_send.at[i], cache_recv.at[i], pair_send.at[6 + i], pair_recv.at[6 + i], pair
        )
        copy.start()
        result.append(copy)
    att_ref[pl.ds(mine, HD), :] = finished(own_q)
    ck_ref[pl.ds(mine, HD), :] = cache[xh, pl.ds(0, HD), :].astype(jnp.bfloat16)
    cv_ref[pl.ds(mine, HD), :] = cache[xh, pl.ds(HD, HD), :].astype(jnp.bfloat16)
    result[0].wait_recv()
    att_ref[pl.ds(theirs, HD), :] = att_recv[...]
    result[1].wait_recv()
    ck_ref[pl.ds(theirs, HD), :] = cache_recv[0]
    result[2].wait_recv()
    cv_ref[pl.ds(theirs, HD), :] = cache_recv[1]

    for copy in exchange + result:
        copy.wait_send()

    def drain(index, carry):
        @pl.when(index < 14)
        def _():
            for direction in range(2):
                ring(direction, z, 0, 0, index + 4, up).wait_send()

        twin_copy(index // 2, index % 2).wait_send()
        return carry

    lax.fori_loop(0, 16, drain, 0)


def attend(query, keys, values, prefix_keys, prefix_values, lens, group, placement, owner):
    vmem = pl.BlockSpec(memory_space=pltpu.VMEM)
    smem = pl.BlockSpec(memory_space=pltpu.SMEM)
    shape = jax.ShapeDtypeStruct((KV, ROWS), jnp.bfloat16)
    dma = pltpu.SemaphoreType.DMA
    return pl.pallas_call(
        attention_kernel,
        out_shape=(shape, shape, shape),
        in_specs=[smem, smem, smem] + [vmem] * 6,
        out_specs=(vmem, vmem, vmem),
        scratch_shapes=[
            pltpu.VMEM((NZ, 2, AUG, LANES), jnp.bfloat16),
            pltpu.VMEM((HD, ROWS), jnp.bfloat16),
            pltpu.VMEM((QN, HD), jnp.bfloat16),
            pltpu.VMEM((QN, 128), jnp.int32),
            pltpu.VMEM((QN, 128), jnp.int32),
            pltpu.VMEM((QN, 128), jnp.int32),
            pltpu.VMEM((QN, 128), jnp.float32),
            pltpu.VMEM((QN, HD + 16), jnp.float32),
            pltpu.VMEM((2, KV, ROWS), jnp.float32),
            pltpu.VMEM((HD, ROWS), jnp.bfloat16),
            pltpu.VMEM((2, HD, ROWS), jnp.bfloat16),
            pltpu.VMEM((HD, ROWS), jnp.bfloat16),
            pltpu.VMEM((2, HD, ROWS), jnp.bfloat16),
            dma((2, 18)),
            dma((2, 18)),
            dma((16,)),
            dma((16,)),
            dma((8,)),
            dma((8,)),
        ],
        compiler_params=pltpu.CompilerParams(
            collective_id=0, has_side_effects=True, vmem_limit_bytes=48 * 1024 * 1024
        ),
    )(
        lens,
        group,
        owner,
        placement.reshape(64, 128),
        query.T,
        keys.T,
        values.T,
        prefix_keys.T,
        prefix_values.T,
    )


def shards(
    query,
    keys,
    values,
    prefix_keys,
    prefix_values,
    residual,
    out_weight,
    suffix_lens,
    req_group,
    placement,
    prefix_owner,
):
    attended, cache_keys, cache_values = attend(
        query,
        keys,
        values,
        prefix_keys,
        prefix_values,
        suffix_lens,
        req_group,
        placement,
        prefix_owner,
    )
    term = jnp.dot(attended.T, out_weight, preferred_element_type=jnp.float32)
    summed = lax.psum_scatter(
        term.astype(jnp.bfloat16), "tp", scatter_dimension=1, tiled=True
    ).astype(jnp.float32)
    hidden = (residual.astype(jnp.float32) + summed).astype(jnp.bfloat16)
    return (hidden, cache_keys.T, cache_values.T)


def solution(mesh):
    return jax.shard_map(
        shards,
        mesh=mesh,
        in_specs=(
            P("seq", "tp"),
            P("seq", "tp"),
            P("seq", "tp"),
            P("seq", "tp"),
            P("seq", "tp"),
            P("seq", "tp"),
            P("tp", None),
            P(),
            P(),
            P(),
            P(),
        ),
        out_specs=(P("seq", "tp"), P("seq", "tp"), P("seq", "tp")),
        check_vma=False,
    )
```

```python
import functools
import math

import jax
import jax.numpy as jnp
from jax import lax
from jax.experimental import pallas as pl
from jax.experimental.pallas import tpu as pltpu
from jax.sharding import PartitionSpec as P

HD = 224
HALF = HD // 2
ROWS = 256
PBLK = 128
PART = ROWS + PBLK
LANES = 2 * PART
QN = 2 * ROWS
KV = 2 * HD
NZ = 8
TP = 8
D = 3584
TQ = 256
NEG = -1e30
COEF = math.log2(math.e) / math.sqrt(HD)
MESH = pl.DeviceIdType.MESH
NT = (((1,), (1,)), ((), ()))
BF = jnp.bfloat16
F32 = jnp.float32


def dot(a, b):
    return jnp.dot(a, b, preferred_element_type=F32)


def dot_nt(a, b):
    return lax.dot_general(a, b, NT, preferred_element_type=F32)


def step_kernel(
    lens_hbm,
    group_hbm,
    owner_hbm,
    pos_hbm,
    q_hbm,
    k_hbm,
    v_hbm,
    pk_hbm,
    pv_hbm,
    res_hbm,
    w_hbm,
    hid_ref,
    ck_ref,
    cv_ref,
    lens_ref,
    group_ref,
    owner_ref,
    pos_ref,
    res_ref,
    w_ref,
    q_own,
    q_other,
    keys,
    vals0,
    vals1,
    weights_ref,
    hot_ref,
    tops,
    q_rows,
    q_pos,
    q_start,
    q_grp,
    top,
    accum,
    cache_k,
    cache_v,
    swap_out,
    swap_in,
    w_send,
    w_all,
    att_out,
    att_all,
    projected,
    local_sem,
    ring_send,
    ring_recv,
    twin_send,
    twin_recv,
    pair_send,
    pair_recv,
    w_send_sem,
    w_recv_sem,
    w_twin_send,
    w_twin_recv,
    att_send_sem,
    att_recv_sem,
):
    seq = lax.axis_index("seq")
    tp = lax.axis_index("tp")
    z = seq // 4
    xh = (seq // 2) % 2
    core = seq % 2
    other = 1 - xh
    twin = 1 - core

    def dev(zz, xx, cc, tt):
        return (zz * 4 + xx * 2 + cc, tt)

    up = dev(lax.rem(z + 1, NZ), xh, core, tp)
    down = dev(lax.rem(z + NZ - 1, NZ), xh, core, tp)
    pair = dev(z, other, core, tp)
    sibling = dev(z, xh, twin, tp)

    def plane(e):
        return lax.rem(xh + e // TP, 2), lax.rem(tp + e, TP)

    mine = pl.multiple_of(xh * HD, 32)
    theirs = pl.multiple_of(other * HD, 32)
    mine_lane = pl.multiple_of(xh * PART, 128)

    blocks = (keys, vals0, vals1)
    heights = (HD, HALF, HALF)
    offsets = (0, 0, HALF)
    suffix = (k_hbm, v_hbm, v_hbm)
    prefix = (pk_hbm, pv_hbm, pv_hbm)

    def landing(f, lane, width):
        at = pl.multiple_of(mine_lane + lane, 128)
        return blocks[f].at[z, core, pl.ds(0, heights[f]), pl.ds(at, width)]

    def rows_of(ref, f, base):
        return ref.at[pl.ds(pl.multiple_of(base + offsets[f], 16), heights[f])]

    own = []
    for f in range(3):
        own.append(
            (
                pltpu.make_async_copy(
                    rows_of(suffix[f], f, mine), landing(f, 0, ROWS), local_sem.at[2 * f]
                ),
                pltpu.make_async_copy(
                    rows_of(prefix[f], f, mine), landing(f, ROWS, PBLK), local_sem.at[2 * f + 1]
                ),
            )
        )
    small = [
        pltpu.make_async_copy(src, dst, local_sem.at[6 + i])
        for i, (src, dst) in enumerate(
            (
                (lens_hbm, lens_ref),
                (group_hbm, group_ref),
                (owner_hbm, owner_ref),
                (pos_hbm, pos_ref),
                (q_hbm.at[pl.ds(mine, HD)], q_own),
                (w_hbm.at[pl.ds(pl.multiple_of(core * HD, 32), HD)], w_ref),
                (res_hbm, res_ref),
            )
        )
    ]
    for copy in own[0] + own[1]:
        copy.start()
    for copy in small[:5]:
        copy.start()
    for copy in own[2]:
        copy.start()
    for copy in small[5:]:
        copy.start()

    barrier = pltpu.get_barrier_semaphore()
    for peer in (up, down, sibling):
        pl.semaphore_signal(barrier, inc=1, device_id=peer, device_id_type=MESH)

    def greet(e, carry):
        xx, tt = plane(e)
        pl.semaphore_signal(barrier, inc=1, device_id=dev(z, xx, core, tt), device_id_type=MESH)
        return carry

    lax.fori_loop(1, 2 * TP, greet, 0)
    pl.semaphore_wait(barrier, 2 * TP + 2)

    def remote(src, dst, send, recv, device):
        return pltpu.make_async_remote_copy(
            src_ref=src,
            dst_ref=dst,
            send_sem=send,
            recv_sem=recv,
            device_id=device,
            device_id_type=MESH,
        )

    def pair_copy(src, dst, i):
        return remote(src, dst, pair_send.at[i], pair_recv.at[i], pair)

    exchange = [
        (
            pair_copy(rows_of(suffix[f], f, theirs), landing(f, 0, ROWS), 2 * f),
            pair_copy(rows_of(prefix[f], f, theirs), landing(f, ROWS, PBLK), 2 * f + 1),
        )
        for f in range(3)
    ]
    exchange_q = pair_copy(q_hbm.at[pl.ds(theirs, HD)], q_other, 6)

    def block(f, slot, cc, part):
        lane = pl.multiple_of(part * PART, 128)
        return blocks[f].at[slot, cc, pl.ds(0, heights[f]), pl.ds(lane, PART)]

    def ring(f, direction, slot, part, n):
        ref = block(f, slot, core, part)
        index = f * 8 + n
        return remote(
            ref,
            ref,
            ring_send.at[direction, index],
            ring_recv.at[direction, index],
            down if direction else up,
        )

    def twin_copy(f, slot, part, cc):
        ref = block(f, slot, cc, part)
        index = f * 16 + slot * 2 + part
        return remote(ref, ref, twin_send.at[index], twin_recv.at[index], sibling)

    def send_own(f, part, n):
        ring(f, 0, z, part, n).start()
        ring(f, 1, z, part, n).start()
        twin_copy(f, z, part, core).start()

    for copy in exchange[0]:
        copy.start()
    for copy in own[0]:
        copy.wait()
    send_own(0, xh, 0)
    exchange_q.start()
    for f in (1, 2):
        for copy in exchange[f]:
            copy.start()
    for copy in own[1]:
        copy.wait()
    send_own(1, xh, 0)

    for copy in small[:5]:
        copy.wait()
    lane_ids = lax.broadcasted_iota(jnp.int32, (128, 128), 1)
    row_ids = lax.broadcasted_iota(jnp.int32, (128, 128), 0)
    for half in range(2):
        source = z * 4 + half * 2 + core
        for piece in range(2):
            row = pos_ref[pl.ds(source * 2 + piece, 1), :]
            spread = jnp.where(lane_ids == row_ids, jnp.broadcast_to(row, (128, 128)), 0)
            column = jnp.sum(spread.astype(F32), axis=1, keepdims=True)
            q_pos[pl.ds(half * ROWS + piece * 128, 128), :] = jnp.broadcast_to(
                column.astype(jnp.int32), (128, 128)
            )
    position = q_pos[...]
    start = jnp.zeros_like(position)
    group = jnp.full_like(position, group_ref[0])
    end = jnp.int32(0)
    for r in range(15):
        end = end + lens_ref[r]
        past = position >= end
        start = jnp.where(past, end, start)
        group = jnp.where(past, group_ref[r + 1], group)
    q_start[...] = start
    q_grp[...] = group
    own_q = pl.multiple_of(xh * ROWS, ROWS)
    other_q = pl.multiple_of(other * ROWS, ROWS)
    q_rows[pl.ds(own_q, ROWS), :] = jnp.transpose(q_own[...].astype(F32)).astype(BF)

    for copy in exchange[0]:
        copy.wait_recv()
    send_own(0, other, 1)
    top[...] = jnp.full_like(top, NEG)
    accum[...] = jnp.zeros_like(accum)
    cache_k[...] = jnp.zeros_like(cache_k)
    cache_v[...] = jnp.zeros_like(cache_v)
    ones = jnp.ones((16, LANES), BF)
    for slot in range(NZ):
        for cc in range(2):
            vals0[slot, cc, pl.ds(HALF, 16), :] = ones
    exchange_q.wait_recv()
    q_rows[pl.ds(other_q, ROWS), :] = jnp.transpose(q_other[...].astype(F32)).astype(BF)

    packed = lax.broadcasted_iota(jnp.int32, (ROWS, 128), 0) + (z * 4 + core) * ROWS

    def slot_at(u):
        k = (u + 1) // 2
        return lax.rem(z + jnp.where(u % 2 == 1, NZ - k, k), NZ)

    def arrived(f, slot):
        for part in range(2):
            twin_copy(f, slot, part, twin).wait_recv()

    def each_unit(f, lo, hi, body):
        def visit(i, carry):
            u = i // 2
            from_twin = i % 2
            slot = slot_at(u)

            @pl.when(from_twin == 1)
            def _():
                arrived(f, slot)

            cc = jnp.where(from_twin == 1, twin, core)
            body(slot, cc, slot * 2 + cc)
            return carry

        lax.fori_loop(lo * 2, hi * 2, visit, 0)

    def score_unit(slot, cc, unit):
        def tile(step, carry):
            rows = pl.ds(pl.multiple_of(step * TQ, TQ), TQ)
            scores = dot(q_rows[rows, :], keys[slot, cc])
            position = q_pos[rows, :]
            start = q_start[rows, :]
            group = q_grp[rows, :]
            pieces = []
            for part in range(2):
                source = slot * 4 + part * 2 + cc
                for piece in range(2):
                    at = part * PART + piece * 128
                    where = pos_ref[pl.ds(source * 2 + piece, 1), :]
                    seen = (where <= position) & (where >= start)
                    pieces.append(jnp.where(seen, scores[:, at : at + 128], NEG))
                at = part * PART + ROWS
                pieces.append(
                    jnp.where(group == owner_ref[source], scores[:, at : at + 128], NEG)
                )
            scores = jnp.concatenate(pieces, axis=1)
            fresh = jnp.maximum(top[rows, :], jnp.max(scores, axis=1, keepdims=True))
            top[rows, :] = fresh
            tops[unit, rows, :] = fresh
            weights_ref[unit, rows, :] = jnp.exp2(
                (scores - jnp.tile(fresh, (1, LANES // 128))) * COEF
            ).astype(BF)
            return carry

        lax.fori_loop(0, QN // TQ, tile, 0)

        for part in range(2):
            source = slot * 4 + part * 2 + cc
            for half in range(2):
                hot = [
                    jnp.where(
                        pos_ref[pl.ds(source * 2 + piece, 1), :] == packed + half * 2 * ROWS,
                        1.0,
                        0.0,
                    ).astype(BF)
                    for piece in range(2)
                ]
                hot_ref[unit, pl.ds(half * ROWS, ROWS), pl.ds(part * ROWS, ROWS)] = (
                    jnp.concatenate(hot, axis=1)
                )
        cache_k[...] += moved(keys, HD, slot, cc, unit)

    def moved(ref, height, slot, cc, unit):
        total = None
        for part in range(2):
            term = dot_nt(
                ref[slot, cc, pl.ds(0, height), pl.ds(part * PART, ROWS)],
                hot_ref[unit, :, pl.ds(part * ROWS, ROWS)],
            )
            total = term if total is None else total + term
        return total

    def value_unit(f, slot, cc, unit):
        ref = blocks[f]
        which = f - 1
        factor = jnp.exp2((tops[unit, :, pl.ds(0, 128)] - top[...]) * COEF)
        width = ref.shape[2]
        added = dot_nt(weights_ref[unit], ref[slot, cc])
        accum[which, :, pl.ds(0, width)] = (
            accum[which, :, pl.ds(0, width)] + added * factor[:, :width]
        )
        cache_v[which] = cache_v[which] + moved(ref, HALF, slot, cc, unit)

    def service(f, n):
        k = n // 2 + 1
        below = lax.rem(z + NZ - k, NZ)
        above = lax.rem(z + k, NZ)
        even = n % 2 == 0
        part = jnp.where(even, xh, other)
        part_above = jnp.where(n == 6, other, part)
        ring(f, 0, below, part, n).wait_recv()

        @pl.when(n < 5)
        def _():
            ring(f, 0, below, part, n + 2).start()

        ring(f, 1, above, part_above, n).wait_recv()

        @pl.when((n < 4) | (n == 5))
        def _():
            ring(f, 1, above, part, n + 2 - n // 5).start()

        twin_copy(f, below, part, core).start()
        twin_copy(f, above, part_above, core).start()

    def prepare_weights():
        small[5].wait()
        for t in range(TP):
            for half in range(2):
                w_send[t, :, pl.ds(half * 128, HALF)] = jnp.transpose(
                    w_ref[pl.ds(half * HALF, HALF), pl.ds(t * KV, KV)].astype(F32)
                ).astype(BF)

        def send(e, carry):
            w_copy(e).start()
            return carry

        lax.fori_loop(1, TP, send, 0)
        w_all[2 * tp + core] = w_send[tp]
        w_twin(0, core).start()

    def w_copy(e):
        to = lax.rem(tp + e, TP)
        return remote(
            w_send.at[to],
            w_all.at[2 * tp + core],
            w_send_sem.at[e],
            w_recv_sem.at[e],
            dev(z, xh, core, to),
        )

    def w_arrival(e):
        head = 2 * lax.rem(tp + TP - e, TP) + core
        return remote(
            w_all.at[head], w_all.at[head], w_send_sem.at[e], w_recv_sem.at[e], sibling
        )

    def w_twin(e, cc):
        head = 2 * lax.rem(tp + TP - e, TP) + cc
        return remote(
            w_all.at[head], w_all.at[head], w_twin_send.at[e], w_twin_recv.at[e], sibling
        )

    def share_weights():
        def share(e, carry):
            w_arrival(e).wait_recv()
            w_twin(e, core).start()
            return carry

        lax.fori_loop(1, TP, share, 0)

    swaps = []

    def swap(i, index):
        height = HD if i == 0 else HALF
        base = (0, HD, HD + HALF)[i]
        rows = pl.ds(base, height)
        return pair_copy(swap_out.at[rows], swap_in.at[rows], 7 + i)

    def send_cache(i, ref):
        height = HD if i == 0 else HALF
        base = (0, HD, HD + HALF)[i]
        out = ck_ref if i == 0 else cv_ref
        offset = (0, 0, HALF)[i]

        @pl.when(xh == 0)
        def _():
            swap_out[pl.ds(base, height), :] = ref[:, ROWS:].astype(BF)
            out[pl.ds(offset, height), :] = ref[:, :ROWS].astype(BF)

        @pl.when(xh == 1)
        def _():
            swap_out[pl.ds(base, height), :] = ref[:, :ROWS].astype(BF)
            out[pl.ds(HD + offset, height), :] = ref[:, ROWS:].astype(BF)

        swap(i, 0).start()

    def att_copy(half, e):
        xx, tt = plane(e)
        return remote(
            att_out.at[half, xx],
            att_all.at[half, 2 * tp + xh],
            att_send_sem.at[half * 16 + e],
            att_recv_sem.at[half * 16 + e],
            dev(z, xx, core, tt),
        )

    def att_head(e):
        return 2 * lax.rem(tp + 2 * TP - e, TP) + lax.rem(xh + e // TP, 2)

    def att_arrival(half, e):
        head = att_head(e)
        return remote(
            att_all.at[half, head],
            att_all.at[half, head],
            att_send_sem.at[half * 16 + e],
            att_recv_sem.at[half * 16 + e],
            sibling,
        )

    def finish(half):
        scaled = accum[half, :, pl.ds(0, HALF)] / accum[0, :, pl.ds(HALF, 1)]
        turned = jnp.transpose(scaled).astype(BF)
        att_out[half, 0] = turned[:, :ROWS]
        att_out[half, 1] = turned[:, ROWS:]

        def send(e, carry):
            att_copy(half, e).start()
            return carry

        lax.fori_loop(1, 2 * TP, send, 0)
        att_all[half, 2 * tp + xh] = att_out[half, xh]

    def project(half):
        def add(e, carry):
            @pl.when(e > 0)
            def _():
                att_arrival(half, e).wait_recv()

            head = att_head(e)
            projected[...] += dot(
                w_all[head, :, pl.ds(half * 128, HALF)], att_all[half, head]
            )
            return carry

        lax.fori_loop(0, 2 * TP, add, 0)

    def key_step(n, carry):
        service(0, n)

        @pl.when(n == 1)
        def _():
            prepare_weights()

        @pl.when(n == 5)
        def _():
            for copy in exchange[1]:
                copy.wait_recv()
            send_own(1, other, 1)

        lo = jnp.where(n == 0, 0, jnp.maximum(n - 1, 1))
        each_unit(0, lo, jnp.maximum(n, 1), score_unit)
        return carry

    lax.fori_loop(0, 7, key_step, 0)

    def first_step(n, carry):
        service(1, n)

        @pl.when(n == 2)
        def _():
            send_cache(0, cache_k)
            share_weights()

        @pl.when(n == 5)
        def _():
            for copy in own[2]:
                copy.wait()
            send_own(2, xh, 0)
            for copy in exchange[2]:
                copy.wait_recv()
            send_own(2, other, 1)

        @pl.when(n < 2)
        def _():
            each_unit(0, n + 6, n + 7, score_unit)

        @pl.when(n >= 2)
        def _():
            each_unit(1, n - 2, n - 1, functools.partial(value_unit, 1))

        return carry

    lax.fori_loop(0, 7, first_step, 0)

    def second_step(n, carry):
        service(2, n)

        @pl.when(n < 2)
        def _():
            each_unit(1, 5 + 2 * n, 7 + n, functools.partial(value_unit, 1))

        @pl.when(n == 1)
        def _():
            finish(0)
            send_cache(1, cache_v.at[0])

        lo = jnp.where(n < 3, 0, 2 * n - 5)
        hi = jnp.where(n == 6, 7, jnp.where(n < 2, 0, 2 * n - 3))
        each_unit(2, lo, hi, functools.partial(value_unit, 2))
        return carry

    lax.fori_loop(0, 7, second_step, 0)
    each_unit(2, 7, 8, functools.partial(value_unit, 2))
    finish(1)
    send_cache(2, cache_v.at[1])

    for e in range(TP):
        w_twin(e, twin).wait_recv()
    small[6].wait()
    projected[...] = res_ref[...].astype(F32)
    project(0)
    for i in range(3):
        swap(i, 0).wait_recv()
    for i, out in enumerate((ck_ref, cv_ref, cv_ref)):
        height = HD if i == 0 else HALF
        base = (0, HD, HD + HALF)[i]
        offset = (0, 0, HALF)[i]
        out[pl.ds(pl.multiple_of(theirs + offset, 16), height), :] = swap_in[
            pl.ds(base, height), :
        ]
    project(1)
    hid_ref[...] = projected[...].astype(BF)

    for f in range(3):
        for copy in exchange[f]:
            copy.wait_send()
        swap(f, 0).wait_send()

        def drain(n, carry, f=f):
            ring(f, 0, z, 0, n).wait_send()
            ring(f, 1, z, 0, n).wait_send()
            return carry

        lax.fori_loop(0, 7, drain, 0)

        def drain_twin(n, carry, f=f):
            twin_copy(f, n // 2, n % 2, core).wait_send()
            return carry

        lax.fori_loop(0, 16, drain_twin, 0)
    exchange_q.wait_send()

    def drain_weights(e, carry):
        @pl.when(e > 0)
        def _():
            w_copy(e).wait_send()

        w_twin(e, core).wait_send()
        return carry

    lax.fori_loop(0, TP, drain_weights, 0)

    def drain_att(e, carry):
        att_copy(0, e).wait_send()
        att_copy(1, e).wait_send()
        return carry

    lax.fori_loop(1, 2 * TP, drain_att, 0)


def whole_step(*operands):
    vmem = pl.BlockSpec(memory_space=pltpu.VMEM)
    hbm = pl.BlockSpec(memory_space=pl.ANY)
    shape = jax.ShapeDtypeStruct((KV, ROWS), BF)
    dma = pltpu.SemaphoreType.DMA
    buffer = pltpu.VMEM
    return pl.pallas_call(
        step_kernel,
        out_shape=(shape, shape, shape),
        in_specs=[hbm] * 11,
        out_specs=(vmem, vmem, vmem),
        scratch_shapes=[
            pltpu.SMEM((16,), jnp.int32),
            pltpu.SMEM((16,), jnp.int32),
            pltpu.SMEM((32,), jnp.int32),
            buffer((64, 128), jnp.int32),
            buffer((KV, ROWS), BF),
            buffer((HD, D), BF),
            buffer((HD, ROWS), BF),
            buffer((HD, ROWS), BF),
            buffer((NZ, 2, HD, LANES), BF),
            buffer((NZ, 2, HALF + 16, LANES), BF),
            buffer((NZ, 2, HALF, LANES), BF),
            buffer((2 * NZ, QN, LANES), BF),
            buffer((2 * NZ, QN, QN), BF),
            buffer((2 * NZ, QN, 128), F32),
            buffer((QN, HD), BF),
            buffer((QN, 128), jnp.int32),
            buffer((QN, 128), jnp.int32),
            buffer((QN, 128), jnp.int32),
            buffer((QN, 128), F32),
            buffer((2, QN, 128), F32),
            buffer((HD, QN), F32),
            buffer((2, HALF, QN), F32),
            buffer((KV, ROWS), BF),
            buffer((KV, ROWS), BF),
            buffer((TP, KV, 256), BF),
            buffer((2 * TP, KV, 256), BF),
            buffer((2, 2, HALF, ROWS), BF),
            buffer((2, 2 * TP, HALF, ROWS), BF),
            buffer((KV, ROWS), F32),
            dma((13,)),
            dma((2, 24)),
            dma((2, 24)),
            dma((48,)),
            dma((48,)),
            dma((10,)),
            dma((10,)),
            dma((TP,)),
            dma((TP,)),
            dma((TP,)),
            dma((TP,)),
            dma((32,)),
            dma((32,)),
        ],
        compiler_params=pltpu.CompilerParams(
            collective_id=0, has_side_effects=True, vmem_limit_bytes=60 * 1024 * 1024
        ),
    )(*operands)


def shards(
    query,
    keys,
    values,
    prefix_keys,
    prefix_values,
    residual,
    out_weight,
    suffix_lens,
    req_group,
    placement,
    prefix_owner,
):
    hidden, cache_keys, cache_values = whole_step(
        suffix_lens,
        req_group,
        prefix_owner,
        placement.reshape(64, 128),
        query.T,
        keys.T,
        values.T,
        prefix_keys.T,
        prefix_values.T,
        residual.T,
        out_weight,
    )
    return (hidden.T, cache_keys.T, cache_values.T)


def solution(mesh):
    return jax.shard_map(
        shards,
        mesh=mesh,
        in_specs=(
            P("seq", "tp"),
            P("seq", "tp"),
            P("seq", "tp"),
            P("seq", "tp"),
            P("seq", "tp"),
            P("seq", "tp"),
            P("tp", None),
            P(),
            P(),
            P(),
            P(),
        ),
        out_specs=(P("seq", "tp"), P("seq", "tp"), P("seq", "tp")),
        check_vma=False,
    )
```

```python
import functools
import math

import jax
import jax.numpy as jnp
from jax import lax
from jax.experimental import pallas as pl
from jax.experimental.pallas import tpu as pltpu
from jax.sharding import PartitionSpec as P

HD = 224
HALF = HD // 2
ROWS = 256
PBLK = 128
PART = ROWS + PBLK
LANES = 2 * PART
QN = 2 * ROWS
KV = 2 * HD
NZ = 8
TP = 8
D = 3584
TQ = 256
NEG = -1e30
COEF = math.log2(math.e) / math.sqrt(HD)
MESH = pl.DeviceIdType.MESH
NT = (((1,), (1,)), ((), ()))
BF = jnp.bfloat16
F32 = jnp.float32


def dot(a, b):
    return jnp.dot(a, b, preferred_element_type=F32)


def dot_nt(a, b):
    return lax.dot_general(a, b, NT, preferred_element_type=F32)


def step_kernel(
    lens_hbm,
    group_hbm,
    owner_hbm,
    pos_hbm,
    q_hbm,
    k_hbm,
    v_hbm,
    pk_hbm,
    pv_hbm,
    res_hbm,
    w_hbm,
    out_ref,
    lens_ref,
    group_ref,
    owner_ref,
    pos_ref,
    res_ref,
    w_ref,
    q_own,
    q_other,
    keys,
    vals0,
    vals1,
    weights_ref,
    hot_ref,
    tops,
    q_rows,
    q_pos,
    q_start,
    q_grp,
    top,
    accum,
    cache_k,
    cache_v,
    swap_out,
    swap_in,
    w_send,
    w_all,
    att_out,
    att_all,
    projected,
    local_sem,
    ring_send,
    ring_recv,
    twin_send,
    twin_recv,
    pair_send,
    pair_recv,
    w_send_sem,
    w_recv_sem,
    w_twin_send,
    w_twin_recv,
    att_send_sem,
    att_recv_sem,
):
    hid_ref, ck_ref, cv_ref = (out_ref.at[pl.ds(i * KV, KV)] for i in range(3))
    seq = lax.axis_index("seq")
    tp = lax.axis_index("tp")
    z = seq // 4
    xh = (seq // 2) % 2
    core = seq % 2
    other = 1 - xh
    twin = 1 - core

    def dev(zz, xx, cc, tt):
        return (zz * 4 + xx * 2 + cc, tt)

    up = dev(lax.rem(z + 1, NZ), xh, core, tp)
    down = dev(lax.rem(z + NZ - 1, NZ), xh, core, tp)
    pair = dev(z, other, core, tp)
    sibling = dev(z, xh, twin, tp)

    def plane(e):
        return lax.rem(xh + e // TP, 2), lax.rem(tp + e, TP)

    mine = pl.multiple_of(xh * HD, 32)
    theirs = pl.multiple_of(other * HD, 32)
    mine_lane = pl.multiple_of(xh * PART, 128)

    blocks = (keys, vals0, vals1)
    heights = (HD, HALF, HALF)
    offsets = (0, 0, HALF)
    suffix = (k_hbm, v_hbm, v_hbm)
    prefix = (pk_hbm, pv_hbm, pv_hbm)

    def landing(f, lane, width):
        at = pl.multiple_of(mine_lane + lane, 128)
        return blocks[f].at[z, core, pl.ds(0, heights[f]), pl.ds(at, width)]

    def rows_of(ref, f, base):
        return ref.at[pl.ds(pl.multiple_of(base + offsets[f], 16), heights[f])]

    own = []
    for f in range(3):
        own.append(
            (
                pltpu.make_async_copy(
                    rows_of(suffix[f], f, mine), landing(f, 0, ROWS), local_sem.at[2 * f]
                ),
                pltpu.make_async_copy(
                    rows_of(prefix[f], f, mine), landing(f, ROWS, PBLK), local_sem.at[2 * f + 1]
                ),
            )
        )
    small = [
        pltpu.make_async_copy(src, dst, local_sem.at[6 + i])
        for i, (src, dst) in enumerate(
            (
                (lens_hbm, lens_ref),
                (group_hbm, group_ref),
                (owner_hbm, owner_ref),
                (pos_hbm, pos_ref),
                (q_hbm.at[pl.ds(mine, HD)], q_own),
                (w_hbm.at[pl.ds(pl.multiple_of(core * HD, 32), HD)], w_ref),
                (res_hbm, res_ref),
            )
        )
    ]
    for copy in own[0] + own[1]:
        copy.start()
    for copy in small[:5]:
        copy.start()
    for copy in own[2]:
        copy.start()
    for copy in small[5:]:
        copy.start()

    barrier = pltpu.get_barrier_semaphore()
    for peer in (up, down, sibling):
        pl.semaphore_signal(barrier, inc=1, device_id=peer, device_id_type=MESH)

    def greet(e, carry):
        xx, tt = plane(e)
        pl.semaphore_signal(barrier, inc=1, device_id=dev(z, xx, core, tt), device_id_type=MESH)
        return carry

    lax.fori_loop(1, 2 * TP, greet, 0)
    pl.semaphore_wait(barrier, 2 * TP + 2)

    def remote(src, dst, send, recv, device):
        return pltpu.make_async_remote_copy(
            src_ref=src,
            dst_ref=dst,
            send_sem=send,
            recv_sem=recv,
            device_id=device,
            device_id_type=MESH,
        )

    def pair_copy(src, dst, i):
        return remote(src, dst, pair_send.at[i], pair_recv.at[i], pair)

    exchange = [
        (
            pair_copy(rows_of(suffix[f], f, theirs), landing(f, 0, ROWS), 2 * f),
            pair_copy(rows_of(prefix[f], f, theirs), landing(f, ROWS, PBLK), 2 * f + 1),
        )
        for f in range(3)
    ]
    exchange_q = pair_copy(q_hbm.at[pl.ds(theirs, HD)], q_other, 6)

    def block(f, slot, cc, part):
        lane = pl.multiple_of(part * PART, 128)
        return blocks[f].at[slot, cc, pl.ds(0, heights[f]), pl.ds(lane, PART)]

    def ring(f, direction, slot, part, n):
        ref = block(f, slot, core, part)
        index = f * 8 + n
        return remote(
            ref,
            ref,
            ring_send.at[direction, index],
            ring_recv.at[direction, index],
            down if direction else up,
        )

    def twin_copy(f, slot, part, cc):
        ref = block(f, slot, cc, part)
        index = f * 16 + slot * 2 + part
        return remote(ref, ref, twin_send.at[index], twin_recv.at[index], sibling)

    def send_own(f, part, n):
        ring(f, 0, z, part, n).start()
        ring(f, 1, z, part, n).start()
        twin_copy(f, z, part, core).start()

    for copy in exchange[0]:
        copy.start()
    for copy in own[0]:
        copy.wait()
    send_own(0, xh, 0)
    exchange_q.start()
    for f in (1, 2):
        for copy in exchange[f]:
            copy.start()
    for copy in own[1]:
        copy.wait()
    send_own(1, xh, 0)

    for copy in small[:5]:
        copy.wait()
    lane_ids = lax.broadcasted_iota(jnp.int32, (128, 128), 1)
    row_ids = lax.broadcasted_iota(jnp.int32, (128, 128), 0)
    for half in range(2):
        source = z * 4 + half * 2 + core
        for piece in range(2):
            row = pos_ref[pl.ds(source * 2 + piece, 1), :]
            spread = jnp.where(lane_ids == row_ids, jnp.broadcast_to(row, (128, 128)), 0)
            column = jnp.sum(spread.astype(F32), axis=1, keepdims=True)
            q_pos[pl.ds(half * ROWS + piece * 128, 128), :] = jnp.broadcast_to(
                column.astype(jnp.int32), (128, 128)
            )
    position = q_pos[...]
    start = jnp.zeros_like(position)
    group = jnp.full_like(position, group_ref[0])
    end = jnp.int32(0)
    for r in range(15):
        end = end + lens_ref[r]
        past = position >= end
        start = jnp.where(past, end, start)
        group = jnp.where(past, group_ref[r + 1], group)
    q_start[...] = start
    q_grp[...] = group
    own_q = pl.multiple_of(xh * ROWS, ROWS)
    other_q = pl.multiple_of(other * ROWS, ROWS)
    q_rows[pl.ds(own_q, ROWS), :] = jnp.transpose(q_own[...].astype(F32)).astype(BF)

    for copy in exchange[0]:
        copy.wait_recv()
    send_own(0, other, 1)
    top[...] = jnp.full_like(top, NEG)
    accum[...] = jnp.zeros_like(accum)
    cache_k[...] = jnp.zeros_like(cache_k)
    cache_v[...] = jnp.zeros_like(cache_v)
    ones = jnp.ones((16, LANES), BF)
    for slot in range(NZ):
        for cc in range(2):
            vals0[slot, cc, pl.ds(HALF, 16), :] = ones
    exchange_q.wait_recv()
    q_rows[pl.ds(other_q, ROWS), :] = jnp.transpose(q_other[...].astype(F32)).astype(BF)

    packed = lax.broadcasted_iota(jnp.int32, (ROWS, 128), 0) + (z * 4 + core) * ROWS

    def slot_at(u):
        k = (u + 1) // 2
        return lax.rem(z + jnp.where(u % 2 == 1, NZ - k, k), NZ)

    def arrived(f, slot):
        for part in range(2):
            twin_copy(f, slot, part, twin).wait_recv()

    def each_unit(f, lo, hi, body):
        def visit(i, carry):
            u = i // 2
            from_twin = i % 2
            slot = slot_at(u)

            @pl.when(from_twin == 1)
            def _():
                arrived(f, slot)

            cc = jnp.where(from_twin == 1, twin, core)
            body(slot, cc, slot * 2 + cc)
            return carry

        lax.fori_loop(lo * 2, hi * 2, visit, 0)

    def score_unit(slot, cc, unit):
        def tile(step, carry):
            rows = pl.ds(pl.multiple_of(step * TQ, TQ), TQ)
            scores = dot(q_rows[rows, :], keys[slot, cc])
            position = q_pos[rows, :]
            start = q_start[rows, :]
            group = q_grp[rows, :]
            pieces = []
            for part in range(2):
                source = slot * 4 + part * 2 + cc
                for piece in range(2):
                    at = part * PART + piece * 128
                    where = pos_ref[pl.ds(source * 2 + piece, 1), :]
                    seen = (where <= position) & (where >= start)
                    pieces.append(jnp.where(seen, scores[:, at : at + 128], NEG))
                at = part * PART + ROWS
                pieces.append(
                    jnp.where(group == owner_ref[source], scores[:, at : at + 128], NEG)
                )
            scores = jnp.concatenate(pieces, axis=1)
            fresh = jnp.maximum(top[rows, :], jnp.max(scores, axis=1, keepdims=True))
            top[rows, :] = fresh
            tops[unit, rows, :] = fresh
            weights_ref[unit, rows, :] = jnp.exp2(
                (scores - jnp.tile(fresh, (1, LANES // 128))) * COEF
            ).astype(BF)
            return carry

        lax.fori_loop(0, QN // TQ, tile, 0)

        for part in range(2):
            source = slot * 4 + part * 2 + cc
            for half in range(2):
                hot = [
                    jnp.where(
                        pos_ref[pl.ds(source * 2 + piece, 1), :] == packed + half * 2 * ROWS,
                        1.0,
                        0.0,
                    ).astype(BF)
                    for piece in range(2)
                ]
                hot_ref[unit, pl.ds(half * ROWS, ROWS), pl.ds(part * ROWS, ROWS)] = (
                    jnp.concatenate(hot, axis=1)
                )
        cache_k[...] += moved(keys, HD, slot, cc, unit)

    def moved(ref, height, slot, cc, unit):
        total = None
        for part in range(2):
            term = dot_nt(
                ref[slot, cc, pl.ds(0, height), pl.ds(part * PART, ROWS)],
                hot_ref[unit, :, pl.ds(part * ROWS, ROWS)],
            )
            total = term if total is None else total + term
        return total

    def value_unit(f, slot, cc, unit):
        ref = blocks[f]
        which = f - 1
        factor = jnp.exp2((tops[unit, :, pl.ds(0, 128)] - top[...]) * COEF)
        width = ref.shape[2]
        added = dot_nt(weights_ref[unit], ref[slot, cc])
        accum[which, :, pl.ds(0, width)] = (
            accum[which, :, pl.ds(0, width)] + added * factor[:, :width]
        )
        cache_v[which] = cache_v[which] + moved(ref, HALF, slot, cc, unit)

    def service(f, n):
        k = n // 2 + 1
        below = lax.rem(z + NZ - k, NZ)
        above = lax.rem(z + k, NZ)
        even = n % 2 == 0
        part = jnp.where(even, xh, other)
        part_above = jnp.where(n == 6, other, part)
        ring(f, 0, below, part, n).wait_recv()

        @pl.when(n < 5)
        def _():
            ring(f, 0, below, part, n + 2).start()

        ring(f, 1, above, part_above, n).wait_recv()

        @pl.when((n < 4) | (n == 5))
        def _():
            ring(f, 1, above, part, n + 2 - n // 5).start()

        twin_copy(f, below, part, core).start()
        twin_copy(f, above, part_above, core).start()

    def prepare_weights():
        small[5].wait()
        for t in range(TP):
            for half in range(2):
                w_send[t, :, pl.ds(half * 128, HALF)] = jnp.transpose(
                    w_ref[pl.ds(half * HALF, HALF), pl.ds(t * KV, KV)].astype(F32)
                ).astype(BF)

        def send(e, carry):
            w_copy(e).start()
            return carry

        lax.fori_loop(1, TP, send, 0)
        w_all[2 * tp + core] = w_send[tp]
        w_twin(0, core).start()

    def w_copy(e):
        to = lax.rem(tp + e, TP)
        return remote(
            w_send.at[to],
            w_all.at[2 * tp + core],
            w_send_sem.at[e],
            w_recv_sem.at[e],
            dev(z, xh, core, to),
        )

    def w_arrival(e):
        head = 2 * lax.rem(tp + TP - e, TP) + core
        return remote(
            w_all.at[head], w_all.at[head], w_send_sem.at[e], w_recv_sem.at[e], sibling
        )

    def w_twin(e, cc):
        head = 2 * lax.rem(tp + TP - e, TP) + cc
        return remote(
            w_all.at[head], w_all.at[head], w_twin_send.at[e], w_twin_recv.at[e], sibling
        )

    def share_weights():
        def share(e, carry):
            w_arrival(e).wait_recv()
            w_twin(e, core).start()
            return carry

        lax.fori_loop(1, TP, share, 0)

    swaps = []

    def swap(i, index):
        height = HD if i == 0 else HALF
        base = (0, HD, HD + HALF)[i]
        rows = pl.ds(base, height)
        return pair_copy(swap_out.at[rows], swap_in.at[rows], 7 + i)

    def send_cache(i, ref):
        height = HD if i == 0 else HALF
        base = (0, HD, HD + HALF)[i]
        out = ck_ref if i == 0 else cv_ref
        offset = (0, 0, HALF)[i]

        @pl.when(xh == 0)
        def _():
            swap_out[pl.ds(base, height), :] = ref[:, ROWS:].astype(BF)
            out[pl.ds(offset, height), :] = ref[:, :ROWS].astype(BF)

        @pl.when(xh == 1)
        def _():
            swap_out[pl.ds(base, height), :] = ref[:, :ROWS].astype(BF)
            out[pl.ds(HD + offset, height), :] = ref[:, ROWS:].astype(BF)

        swap(i, 0).start()

    def att_copy(half, e):
        xx, tt = plane(e)
        return remote(
            att_out.at[half, xx],
            att_all.at[half, 2 * tp + xh],
            att_send_sem.at[half * 16 + e],
            att_recv_sem.at[half * 16 + e],
            dev(z, xx, core, tt),
        )

    def att_head(e):
        return 2 * lax.rem(tp + 2 * TP - e, TP) + lax.rem(xh + e // TP, 2)

    def att_arrival(half, e):
        head = att_head(e)
        return remote(
            att_all.at[half, head],
            att_all.at[half, head],
            att_send_sem.at[half * 16 + e],
            att_recv_sem.at[half * 16 + e],
            sibling,
        )

    def finish(half):
        scaled = accum[half, :, pl.ds(0, HALF)] / accum[0, :, pl.ds(HALF, 1)]
        turned = jnp.transpose(scaled).astype(BF)
        att_out[half, 0] = turned[:, :ROWS]
        att_out[half, 1] = turned[:, ROWS:]

        def send(e, carry):
            att_copy(half, e).start()
            return carry

        lax.fori_loop(1, 2 * TP, send, 0)
        att_all[half, 2 * tp + xh] = att_out[half, xh]

    def project(half):
        def add(e, carry):
            @pl.when(e > 0)
            def _():
                att_arrival(half, e).wait_recv()

            head = att_head(e)
            projected[...] += dot(
                w_all[head, :, pl.ds(half * 128, HALF)], att_all[half, head]
            )
            return carry

        lax.fori_loop(0, 2 * TP, add, 0)

    first_values = functools.partial(value_unit, 1)
    second_values = functools.partial(value_unit, 2)

    def round_a(i, carry):
        service(0, i)

        @pl.when(i == 1)
        def _():
            prepare_weights()

        @pl.when(i == 3)
        def _():
            for copy in exchange[1]:
                copy.wait_recv()
            send_own(1, other, 1)

        lo = jnp.where(i == 0, 0, jnp.maximum(i - 1, 1))
        each_unit(0, lo, jnp.maximum(i, 1), score_unit)
        return carry

    lax.fori_loop(0, 4, round_a, 0)

    def round_b(i, carry):
        @pl.when(i < 2)
        def _():
            service(0, i + 4)

        @pl.when(i >= 2)
        def _():
            service(1, i - 2)

        each_unit(0, i + 3, i + 4, score_unit)
        return carry

    lax.fori_loop(0, 4, round_b, 0)

    def round_c(i, carry):
        @pl.when(i == 0)
        def _():
            service(0, 6)
            share_weights()

        @pl.when(i > 0)
        def _():
            service(1, i + 1)

        @pl.when(i == 2)
        def _():
            for copy in own[2]:
                copy.wait()
            send_own(2, xh, 0)
            for copy in exchange[2]:
                copy.wait_recv()
            send_own(2, other, 1)

        @pl.when(i == 1)
        def _():
            each_unit(0, 7, 8, score_unit)

        @pl.when(i == 2)
        def _():
            send_cache(0, cache_k)
            each_unit(1, 0, 1, first_values)

        return carry

    lax.fori_loop(0, 3, round_c, 0)

    def round_d(i, carry):
        @pl.when(i < 4)
        def _():
            @pl.when(i < 2)
            def _():
                service(1, i + 4)

            @pl.when(i >= 2)
            def _():
                service(2, i - 2)

        @pl.when(i == 4)
        def _():
            service(1, 6)

        @pl.when(i > 4)
        def _():
            service(2, i - 3)

        each_unit(1, i + 1, i + 2, first_values)

        @pl.when(i == 6)
        def _():
            finish(0)
            send_cache(1, cache_v.at[0])

        return carry

    lax.fori_loop(0, 7, round_d, 0)

    def round_e(i, carry):
        @pl.when(i < 2)
        def _():
            service(2, i + 4)

        @pl.when(i == 3)
        def _():
            service(2, 6)

        lo = jnp.where(i == 0, 0, jnp.where(i == 3, 7, 3 * i - 1))
        hi = jnp.where(i == 3, 8, jnp.where(i == 2, 7, 3 * i + 2))
        each_unit(2, lo, hi, second_values)
        return carry

    lax.fori_loop(0, 4, round_e, 0)
    finish(1)
    send_cache(2, cache_v.at[1])

    for e in range(TP):
        w_twin(e, twin).wait_recv()
    small[6].wait()
    projected[...] = res_ref[...].astype(F32)
    project(0)
    for i in range(3):
        swap(i, 0).wait_recv()
    for i, out in enumerate((ck_ref, cv_ref, cv_ref)):
        height = HD if i == 0 else HALF
        base = (0, HD, HD + HALF)[i]
        offset = (0, 0, HALF)[i]
        out[pl.ds(pl.multiple_of(theirs + offset, 16), height), :] = swap_in[
            pl.ds(base, height), :
        ]
    project(1)
    hid_ref[...] = projected[...].astype(BF)

    for f in range(3):
        for copy in exchange[f]:
            copy.wait_send()
        swap(f, 0).wait_send()

        def drain(n, carry, f=f):
            ring(f, 0, z, 0, n).wait_send()
            ring(f, 1, z, 0, n).wait_send()
            return carry

        lax.fori_loop(0, 7, drain, 0)

        def drain_twin(n, carry, f=f):
            twin_copy(f, n // 2, n % 2, core).wait_send()
            return carry

        lax.fori_loop(0, 16, drain_twin, 0)
    exchange_q.wait_send()

    def drain_weights(e, carry):
        @pl.when(e > 0)
        def _():
            w_copy(e).wait_send()

        w_twin(e, core).wait_send()
        return carry

    lax.fori_loop(0, TP, drain_weights, 0)

    def drain_att(e, carry):
        att_copy(0, e).wait_send()
        att_copy(1, e).wait_send()
        return carry

    lax.fori_loop(1, 2 * TP, drain_att, 0)


def whole_step(*operands):
    vmem = pl.BlockSpec(memory_space=pltpu.VMEM)
    hbm = pl.BlockSpec(memory_space=pltpu.HBM)
    shape = jax.ShapeDtypeStruct((3 * KV, ROWS), BF)
    dma = pltpu.SemaphoreType.DMA
    buffer = pltpu.VMEM
    return pl.pallas_call(
        step_kernel,
        out_shape=shape,
        in_specs=[hbm] * 11,
        out_specs=vmem,
        scratch_shapes=[
            pltpu.SMEM((16,), jnp.int32),
            pltpu.SMEM((16,), jnp.int32),
            pltpu.SMEM((32,), jnp.int32),
            buffer((64, 128), jnp.int32),
            buffer((KV, ROWS), BF),
            buffer((HD, D), BF),
            buffer((HD, ROWS), BF),
            buffer((HD, ROWS), BF),
            buffer((NZ, 2, HD, LANES), BF),
            buffer((NZ, 2, HALF + 16, LANES), BF),
            buffer((NZ, 2, HALF, LANES), BF),
            buffer((2 * NZ, QN, LANES), BF),
            buffer((2 * NZ, QN, QN), BF),
            buffer((2 * NZ, QN, 128), F32),
            buffer((QN, HD), BF),
            buffer((QN, 128), jnp.int32),
            buffer((QN, 128), jnp.int32),
            buffer((QN, 128), jnp.int32),
            buffer((QN, 128), F32),
            buffer((2, QN, 128), F32),
            buffer((HD, QN), F32),
            buffer((2, HALF, QN), F32),
            buffer((KV, ROWS), BF),
            buffer((KV, ROWS), BF),
            buffer((TP, KV, 256), BF),
            buffer((2 * TP, KV, 256), BF),
            buffer((2, 2, HALF, ROWS), BF),
            buffer((2, 2 * TP, HALF, ROWS), BF),
            buffer((KV, ROWS), F32),
            dma((13,)),
            dma((2, 24)),
            dma((2, 24)),
            dma((48,)),
            dma((48,)),
            dma((10,)),
            dma((10,)),
            dma((TP,)),
            dma((TP,)),
            dma((TP,)),
            dma((TP,)),
            dma((32,)),
            dma((32,)),
        ],
        compiler_params=pltpu.CompilerParams(
            collective_id=0, has_side_effects=True, vmem_limit_bytes=52 * 1024 * 1024
        ),
    )(*[pltpu.with_memory_space_constraint(x, pltpu.HBM) for x in operands])


def shards(
    query,
    keys,
    values,
    prefix_keys,
    prefix_values,
    residual,
    out_weight,
    suffix_lens,
    req_group,
    placement,
    prefix_owner,
):
    out = whole_step(
        suffix_lens,
        req_group,
        prefix_owner,
        placement.reshape(64, 128),
        query.T,
        keys.T,
        values.T,
        prefix_keys.T,
        prefix_values.T,
        residual.T,
        out_weight,
    )
    return (out[:KV].T, out[KV : 2 * KV].T, out[2 * KV :].T)


def solution(mesh):
    return jax.shard_map(
        shards,
        mesh=mesh,
        in_specs=(
            P("seq", "tp"),
            P("seq", "tp"),
            P("seq", "tp"),
            P("seq", "tp"),
            P("seq", "tp"),
            P("seq", "tp"),
            P("tp", None),
            P(),
            P(),
            P(),
            P(),
        ),
        out_specs=(P("seq", "tp"), P("seq", "tp"), P("seq", "tp")),
        check_vma=False,
    )
```

```python
import functools
import math

import jax
import jax.numpy as jnp
from jax import lax
from jax.experimental import pallas as pl
from jax.experimental.pallas import tpu as pltpu
from jax.sharding import PartitionSpec as P

HD = 224
CUT = (128, 96)
CUT_AT = (0, 128)
ROWS = 256
PBLK = 128
PART = ROWS + PBLK
LANES = 2 * PART
QN = 2 * ROWS
KV = 2 * HD
NZ = 8
TP = 8
D = 3584
TQ = 256
NEG = -1e30
COEF = math.log2(math.e) / math.sqrt(HD)
MESH = pl.DeviceIdType.MESH
NT = (((1,), (1,)), ((), ()))
BF = jnp.bfloat16
F32 = jnp.float32


def dot(a, b):
    return jnp.dot(a, b, preferred_element_type=F32)


def dot_nt(a, b):
    return lax.dot_general(a, b, NT, preferred_element_type=F32)


def step_kernel(
    lens_hbm,
    group_hbm,
    owner_hbm,
    pos_hbm,
    q_hbm,
    k_hbm,
    v_hbm,
    pk_hbm,
    pv_hbm,
    res_hbm,
    w_hbm,
    out_ref,
    lens_ref,
    group_ref,
    owner_ref,
    pos_ref,
    res_ref,
    w_ref,
    q_own,
    q_other,
    keys,
    vals0,
    vals1,
    weights_ref,
    hot_ref,
    tops,
    q_rows,
    q_pos,
    q_start,
    q_grp,
    top,
    accum,
    cache_k,
    cache_v,
    swap_out,
    swap_in,
    w_send,
    w_all,
    att_out,
    att_all,
    projected,
    local_sem,
    ring_send,
    ring_recv,
    twin_send,
    twin_recv,
    pair_send,
    pair_recv,
    w_send_sem,
    w_recv_sem,
    w_twin_send,
    w_twin_recv,
    att_send_sem,
    att_recv_sem,
):
    hid_ref, ck_ref, cv_ref = (out_ref.at[pl.ds(i * KV, KV)] for i in range(3))
    seq = lax.axis_index("seq")
    tp = lax.axis_index("tp")
    z = seq // 4
    xh = (seq // 2) % 2
    core = seq % 2
    other = 1 - xh
    twin = 1 - core

    def dev(zz, xx, cc, tt):
        return (zz * 4 + xx * 2 + cc, tt)

    up = dev(lax.rem(z + 1, NZ), xh, core, tp)
    down = dev(lax.rem(z + NZ - 1, NZ), xh, core, tp)
    pair = dev(z, other, core, tp)
    sibling = dev(z, xh, twin, tp)

    def plane(e):
        return lax.rem(xh + e // TP, 2), lax.rem(tp + e, TP)

    mine = pl.multiple_of(xh * HD, 32)
    theirs = pl.multiple_of(other * HD, 32)
    mine_lane = pl.multiple_of(xh * PART, 128)

    blocks = (keys, vals0, vals1)
    heights = (HD,) + CUT
    offsets = (0,) + CUT_AT
    bases = (0, HD, HD + CUT[0])
    suffix = (k_hbm, v_hbm, v_hbm)
    prefix = (pk_hbm, pv_hbm, pv_hbm)

    def landing(f, lane, width):
        at = pl.multiple_of(mine_lane + lane, 128)
        return blocks[f].at[z, core, pl.ds(0, heights[f]), pl.ds(at, width)]

    def rows_of(ref, f, base):
        return ref.at[pl.ds(pl.multiple_of(base + offsets[f], 16), heights[f])]

    own = []
    for f in range(3):
        own.append(
            (
                pltpu.make_async_copy(
                    rows_of(suffix[f], f, mine), landing(f, 0, ROWS), local_sem.at[2 * f]
                ),
                pltpu.make_async_copy(
                    rows_of(prefix[f], f, mine), landing(f, ROWS, PBLK), local_sem.at[2 * f + 1]
                ),
            )
        )
    small = [
        pltpu.make_async_copy(src, dst, local_sem.at[6 + i])
        for i, (src, dst) in enumerate(
            (
                (lens_hbm, lens_ref),
                (group_hbm, group_ref),
                (owner_hbm, owner_ref),
                (pos_hbm, pos_ref),
                (q_hbm.at[pl.ds(mine, HD)], q_own),
                (w_hbm.at[pl.ds(pl.multiple_of(core * HD, 32), HD)], w_ref),
                (res_hbm, res_ref),
            )
        )
    ]
    for copy in own[0] + own[1]:
        copy.start()
    for copy in small[:5]:
        copy.start()
    for copy in own[2]:
        copy.start()
    for copy in small[5:]:
        copy.start()

    barrier = pltpu.get_barrier_semaphore()
    for peer in (up, down, sibling):
        pl.semaphore_signal(barrier, inc=1, device_id=peer, device_id_type=MESH)

    def greet(e, carry):
        xx, tt = plane(e)
        pl.semaphore_signal(barrier, inc=1, device_id=dev(z, xx, core, tt), device_id_type=MESH)
        return carry

    lax.fori_loop(1, 2 * TP, greet, 0)
    pl.semaphore_wait(barrier, 2 * TP + 2)

    def remote(src, dst, send, recv, device):
        return pltpu.make_async_remote_copy(
            src_ref=src,
            dst_ref=dst,
            send_sem=send,
            recv_sem=recv,
            device_id=device,
            device_id_type=MESH,
        )

    def pair_copy(src, dst, i):
        return remote(src, dst, pair_send.at[i], pair_recv.at[i], pair)

    exchange = [
        (
            pair_copy(rows_of(suffix[f], f, theirs), landing(f, 0, ROWS), 2 * f),
            pair_copy(rows_of(prefix[f], f, theirs), landing(f, ROWS, PBLK), 2 * f + 1),
        )
        for f in range(3)
    ]
    exchange_q = pair_copy(q_hbm.at[pl.ds(theirs, HD)], q_other, 6)

    def block(f, slot, cc, part):
        lane = pl.multiple_of(part * PART, 128)
        return blocks[f].at[slot, cc, pl.ds(0, heights[f]), pl.ds(lane, PART)]

    def ring(f, direction, slot, part, n):
        ref = block(f, slot, core, part)
        index = f * 8 + n
        return remote(
            ref,
            ref,
            ring_send.at[direction, index],
            ring_recv.at[direction, index],
            down if direction else up,
        )

    def twin_copy(f, slot, part, cc):
        ref = block(f, slot, cc, part)
        index = f * 16 + slot * 2 + part
        return remote(ref, ref, twin_send.at[index], twin_recv.at[index], sibling)

    def send_own(f, part, n):
        ring(f, 0, z, part, n).start()
        ring(f, 1, z, part, n).start()
        twin_copy(f, z, part, core).start()

    for copy in exchange[0]:
        copy.start()
    for copy in own[0]:
        copy.wait()
    send_own(0, xh, 0)
    exchange_q.start()
    for f in (1, 2):
        for copy in exchange[f]:
            copy.start()
    for copy in own[1]:
        copy.wait()
    send_own(1, xh, 0)
    for copy in own[2]:
        copy.wait()
    send_own(2, xh, 0)

    for copy in small[:5]:
        copy.wait()
    lane_ids = lax.broadcasted_iota(jnp.int32, (128, 128), 1)
    row_ids = lax.broadcasted_iota(jnp.int32, (128, 128), 0)
    for half in range(2):
        source = z * 4 + half * 2 + core
        for piece in range(2):
            row = pos_ref[pl.ds(source * 2 + piece, 1), :]
            spread = jnp.where(lane_ids == row_ids, jnp.broadcast_to(row, (128, 128)), 0)
            column = jnp.sum(spread.astype(F32), axis=1, keepdims=True)
            q_pos[pl.ds(half * ROWS + piece * 128, 128), :] = jnp.broadcast_to(
                column.astype(jnp.int32), (128, 128)
            )
    position = q_pos[...]
    start = jnp.zeros_like(position)
    group = jnp.full_like(position, group_ref[0])
    end = jnp.int32(0)
    for r in range(15):
        end = end + lens_ref[r]
        past = position >= end
        start = jnp.where(past, end, start)
        group = jnp.where(past, group_ref[r + 1], group)
    q_start[...] = start
    q_grp[...] = group
    own_q = pl.multiple_of(xh * ROWS, ROWS)
    other_q = pl.multiple_of(other * ROWS, ROWS)
    q_rows[pl.ds(own_q, ROWS), :] = jnp.transpose(q_own[...].astype(F32)).astype(BF)

    for copy in exchange[0]:
        copy.wait_recv()
    send_own(0, other, 1)
    top[...] = jnp.full_like(top, NEG)
    accum[...] = jnp.zeros_like(accum)
    cache_k[...] = jnp.zeros_like(cache_k)
    cache_v[...] = jnp.zeros_like(cache_v)
    ones = jnp.ones((16, LANES), BF)
    for slot in range(NZ):
        for cc in range(2):
            vals0[slot, cc, pl.ds(CUT[0], 16), :] = ones
    exchange_q.wait_recv()
    q_rows[pl.ds(other_q, ROWS), :] = jnp.transpose(q_other[...].astype(F32)).astype(BF)

    packed = lax.broadcasted_iota(jnp.int32, (ROWS, 128), 0) + (z * 4 + core) * ROWS

    def slot_at(u):
        k = (u + 1) // 2
        return lax.rem(z + jnp.where(u % 2 == 1, NZ - k, k), NZ)

    def arrived(f, slot):
        for part in range(2):
            twin_copy(f, slot, part, twin).wait_recv()

    def each_unit(f, lo, hi, body):
        def visit(i, carry):
            u = i // 2
            from_twin = i % 2
            slot = slot_at(u)

            @pl.when(from_twin == 1)
            def _():
                arrived(f, slot)

            cc = jnp.where(from_twin == 1, twin, core)
            body(slot, cc, slot * 2 + cc)
            return carry

        lax.fori_loop(lo * 2, hi * 2, visit, 0)

    def score_unit(slot, cc, unit):
        def tile(step, carry):
            rows = pl.ds(pl.multiple_of(step * TQ, TQ), TQ)
            scores = dot(q_rows[rows, :], keys[slot, cc])
            position = q_pos[rows, :]
            start = q_start[rows, :]
            group = q_grp[rows, :]
            pieces = []
            for part in range(2):
                source = slot * 4 + part * 2 + cc
                for piece in range(2):
                    at = part * PART + piece * 128
                    where = pos_ref[pl.ds(source * 2 + piece, 1), :]
                    seen = (where <= position) & (where >= start)
                    pieces.append(jnp.where(seen, scores[:, at : at + 128], NEG))
                at = part * PART + ROWS
                pieces.append(
                    jnp.where(group == owner_ref[source], scores[:, at : at + 128], NEG)
                )
            scores = jnp.concatenate(pieces, axis=1)
            fresh = jnp.maximum(top[rows, :], jnp.max(scores, axis=1, keepdims=True))
            top[rows, :] = fresh
            tops[unit, rows, :] = fresh
            weights_ref[unit, rows, :] = jnp.exp2(
                (scores - jnp.tile(fresh, (1, LANES // 128))) * COEF
            ).astype(BF)
            return carry

        lax.fori_loop(0, QN // TQ, tile, 0)

        for part in range(2):
            source = slot * 4 + part * 2 + cc
            for half in range(2):
                hot = [
                    jnp.where(
                        pos_ref[pl.ds(source * 2 + piece, 1), :] == packed + half * 2 * ROWS,
                        1.0,
                        0.0,
                    ).astype(BF)
                    for piece in range(2)
                ]
                hot_ref[unit, pl.ds(half * ROWS, ROWS), pl.ds(part * ROWS, ROWS)] = (
                    jnp.concatenate(hot, axis=1)
                )
        cache_k[...] += moved(keys, HD, slot, cc, unit)

    def moved(ref, height, slot, cc, unit):
        total = None
        for part in range(2):
            term = dot_nt(
                ref[slot, cc, pl.ds(0, height), pl.ds(part * PART, ROWS)],
                hot_ref[unit, :, pl.ds(part * ROWS, ROWS)],
            )
            total = term if total is None else total + term
        return total

    def value_unit(f, slot, cc, unit):
        ref = blocks[f]
        which = f - 1
        factor = jnp.tile(jnp.exp2((tops[unit] - top[...]) * COEF), (1, 2))
        width = ref.shape[2]
        added = dot_nt(weights_ref[unit], ref[slot, cc])
        accum[which, :, pl.ds(0, width)] = (
            accum[which, :, pl.ds(0, width)] + added * factor[:, :width]
        )
        rows = pl.ds(0, CUT[which])
        cache_v[which, rows, :] = cache_v[which, rows, :] + moved(ref, CUT[which], slot, cc, unit)

    def service(f, n):
        k = n // 2 + 1
        below = lax.rem(z + NZ - k, NZ)
        above = lax.rem(z + k, NZ)
        even = n % 2 == 0
        part = jnp.where(even, xh, other)
        part_above = jnp.where(n == 6, other, part)
        ring(f, 0, below, part, n).wait_recv()

        @pl.when(n < 5)
        def _():
            ring(f, 0, below, part, n + 2).start()

        ring(f, 1, above, part_above, n).wait_recv()

        @pl.when((n < 4) | (n == 5))
        def _():
            ring(f, 1, above, part, n + 2 - n // 5).start()

        twin_copy(f, below, part, core).start()
        twin_copy(f, above, part_above, core).start()

    def prepare_weights():
        small[5].wait()
        for t in range(TP):
            for half in range(2):
                w_send[t, :, pl.ds(CUT_AT[half], CUT[half])] = jnp.transpose(
                    w_ref[pl.ds(CUT_AT[half], CUT[half]), pl.ds(t * KV, KV)].astype(F32)
                ).astype(BF)

        def send(e, carry):
            w_copy(e).start()
            return carry

        lax.fori_loop(1, TP, send, 0)
        w_all[2 * tp + core] = w_send[tp]
        w_twin(0, core).start()

    def w_copy(e):
        to = lax.rem(tp + e, TP)
        return remote(
            w_send.at[to],
            w_all.at[2 * tp + core],
            w_send_sem.at[e],
            w_recv_sem.at[e],
            dev(z, xh, core, to),
        )

    def w_arrival(e):
        head = 2 * lax.rem(tp + TP - e, TP) + core
        return remote(
            w_all.at[head], w_all.at[head], w_send_sem.at[e], w_recv_sem.at[e], sibling
        )

    def w_twin(e, cc):
        head = 2 * lax.rem(tp + TP - e, TP) + cc
        return remote(
            w_all.at[head], w_all.at[head], w_twin_send.at[e], w_twin_recv.at[e], sibling
        )

    def share_weights():
        def share(e, carry):
            w_arrival(e).wait_recv()
            w_twin(e, core).start()
            return carry

        lax.fori_loop(1, TP, share, 0)

    swaps = []

    def swap(i, index):
        rows = pl.ds(bases[i], heights[i])
        return pair_copy(swap_out.at[rows], swap_in.at[rows], 7 + i)

    def send_cache(i, ref):
        height, base, offset = heights[i], bases[i], offsets[i]
        out = ck_ref if i == 0 else cv_ref

        @pl.when(xh == 0)
        def _():
            swap_out[pl.ds(base, height), :] = ref[:, ROWS:].astype(BF)
            out[pl.ds(offset, height), :] = ref[:, :ROWS].astype(BF)

        @pl.when(xh == 1)
        def _():
            swap_out[pl.ds(base, height), :] = ref[:, :ROWS].astype(BF)
            out[pl.ds(HD + offset, height), :] = ref[:, ROWS:].astype(BF)

        swap(i, 0).start()

    def att_copy(half, e):
        xx, tt = plane(e)
        return remote(
            att_out.at[half, xx, pl.ds(0, CUT[half])],
            att_all.at[half, 2 * tp + xh, pl.ds(0, CUT[half])],
            att_send_sem.at[half * 16 + e],
            att_recv_sem.at[half * 16 + e],
            dev(z, xx, core, tt),
        )

    def att_head(e):
        return 2 * lax.rem(tp + 2 * TP - e, TP) + lax.rem(xh + e // TP, 2)

    def att_arrival(half, e):
        head = att_head(e)
        return remote(
            att_all.at[half, head, pl.ds(0, CUT[half])],
            att_all.at[half, head, pl.ds(0, CUT[half])],
            att_send_sem.at[half * 16 + e],
            att_recv_sem.at[half * 16 + e],
            sibling,
        )

    def finish(half):
        rows = pl.ds(0, CUT[half])
        scaled = accum[half, :, rows] / accum[0, :, pl.ds(CUT[0], 1)]
        turned = jnp.transpose(scaled).astype(BF)
        att_out[half, 0, rows, :] = turned[:, :ROWS]
        att_out[half, 1, rows, :] = turned[:, ROWS:]

        def send(e, carry):
            att_copy(half, e).start()
            return carry

        lax.fori_loop(1, 2 * TP, send, 0)
        att_all[half, 2 * tp + xh, rows, :] = att_out[half, xh, rows, :]

    def project(half):
        def add(e, carry):
            @pl.when(e > 0)
            def _():
                att_arrival(half, e).wait_recv()

            head = att_head(e)
            projected[...] += dot(
                w_all[head, :, pl.ds(CUT_AT[half], CUT[half])],
                att_all[half, head, pl.ds(0, CUT[half]), :],
            )
            return carry

        lax.fori_loop(0, 2 * TP, add, 0)

    first_values = functools.partial(value_unit, 1)
    second_values = functools.partial(value_unit, 2)

    def round_a(i, carry):
        service(0, i)

        @pl.when(i == 1)
        def _():
            prepare_weights()

        @pl.when(i == 3)
        def _():
            for copy in exchange[1]:
                copy.wait_recv()
            send_own(1, other, 1)

        lo = jnp.where(i == 0, 0, jnp.maximum(i - 1, 1))
        each_unit(0, lo, jnp.maximum(i, 1), score_unit)
        return carry

    lax.fori_loop(0, 4, round_a, 0)

    def round_b(i, carry):
        @pl.when(i < 2)
        def _():
            service(0, i + 4)

        @pl.when(i >= 2)
        def _():
            service(1, i - 2)

        each_unit(0, i + 3, i + 4, score_unit)
        return carry

    lax.fori_loop(0, 4, round_b, 0)

    def round_c(i, carry):
        @pl.when(i == 0)
        def _():
            service(0, 6)

        @pl.when(i > 0)
        def _():
            service(1, i + 1)

        @pl.when(i == 2)
        def _():
            for copy in exchange[2]:
                copy.wait_recv()
            send_own(2, other, 1)

        @pl.when(i == 1)
        def _():
            each_unit(0, 7, 8, score_unit)

        @pl.when(i == 2)
        def _():
            send_cache(0, cache_k)
            each_unit(1, 0, 1, first_values)

        return carry

    lax.fori_loop(0, 3, round_c, 0)

    def round_d(i, carry):
        @pl.when(i < 4)
        def _():
            @pl.when(i < 2)
            def _():
                service(1, i + 4)

            @pl.when(i >= 2)
            def _():
                service(2, i - 2)

        @pl.when(i == 4)
        def _():
            service(1, 6)

        @pl.when(i > 4)
        def _():
            service(2, i - 3)

        lo = jnp.where(i < 2, 2 * i + 1, jnp.minimum(i + 3, 8))
        hi = jnp.where(i < 2, 2 * i + 3, jnp.minimum(i + 4, 8))
        each_unit(1, lo, hi, first_values)

        @pl.when(i == 2)
        def _():
            share_weights()

        @pl.when(i == 4)
        def _():
            finish(0)
            send_cache(1, cache_v.at[0, pl.ds(0, CUT[0])])

        lo = jnp.where(i == 6, 2, 0)
        hi = jnp.where(i == 6, 3, jnp.where(i == 5, 2, 0))
        each_unit(2, lo, hi, second_values)
        return carry

    lax.fori_loop(0, 7, round_d, 0)

    def round_e(i, carry):
        @pl.when(i < 2)
        def _():
            service(2, i + 4)

        @pl.when(i == 3)
        def _():
            service(2, 6)

        lo = i + 3 + i // 3
        hi = i + 4 + i // 2
        each_unit(2, lo, hi, second_values)
        return carry

    lax.fori_loop(0, 4, round_e, 0)
    finish(1)
    send_cache(2, cache_v.at[1, pl.ds(0, CUT[1])])

    for e in range(TP):
        w_twin(e, twin).wait_recv()
    small[6].wait()
    projected[...] = res_ref[...].astype(F32)
    project(0)
    for i in range(3):
        swap(i, 0).wait_recv()
    for i, out in enumerate((ck_ref, cv_ref, cv_ref)):
        height, base, offset = heights[i], bases[i], offsets[i]
        out[pl.ds(pl.multiple_of(theirs + offset, 16), height), :] = swap_in[
            pl.ds(base, height), :
        ]
    for f in range(3):
        for copy in exchange[f]:
            copy.wait_send()
        swap(f, 0).wait_send()

        def drain(n, carry, f=f):
            ring(f, 0, z, 0, n).wait_send()
            ring(f, 1, z, 0, n).wait_send()
            return carry

        lax.fori_loop(0, 7, drain, 0)

        def drain_twin(n, carry, f=f):
            twin_copy(f, n // 2, n % 2, core).wait_send()
            return carry

        lax.fori_loop(0, 16, drain_twin, 0)
    exchange_q.wait_send()

    def drain_weights(e, carry):
        @pl.when(e > 0)
        def _():
            w_copy(e).wait_send()

        w_twin(e, core).wait_send()
        return carry

    lax.fori_loop(0, TP, drain_weights, 0)

    project(1)
    hid_ref[...] = projected[...].astype(BF)

    def drain_att(e, carry):
        att_copy(0, e).wait_send()
        att_copy(1, e).wait_send()
        return carry

    lax.fori_loop(1, 2 * TP, drain_att, 0)


def whole_step(*operands):
    vmem = pl.BlockSpec(memory_space=pltpu.VMEM)
    hbm = pl.BlockSpec(memory_space=pltpu.HBM)
    shape = jax.ShapeDtypeStruct((3 * KV, ROWS), BF)
    dma = pltpu.SemaphoreType.DMA
    buffer = pltpu.VMEM
    return pl.pallas_call(
        step_kernel,
        out_shape=shape,
        in_specs=[hbm] * 11,
        out_specs=vmem,
        scratch_shapes=[
            pltpu.SMEM((16,), jnp.int32),
            pltpu.SMEM((16,), jnp.int32),
            pltpu.SMEM((32,), jnp.int32),
            buffer((64, 128), jnp.int32),
            buffer((KV, ROWS), BF),
            buffer((HD, D), BF),
            buffer((HD, ROWS), BF),
            buffer((HD, ROWS), BF),
            buffer((NZ, 2, HD, LANES), BF),
            buffer((NZ, 2, CUT[0] + 16, LANES), BF),
            buffer((NZ, 2, CUT[1], LANES), BF),
            buffer((2 * NZ, QN, LANES), BF),
            buffer((2 * NZ, QN, QN), BF),
            buffer((2 * NZ, QN, 128), F32),
            buffer((QN, HD), BF),
            buffer((QN, 128), jnp.int32),
            buffer((QN, 128), jnp.int32),
            buffer((QN, 128), jnp.int32),
            buffer((QN, 128), F32),
            buffer((2, QN, 256), F32),
            buffer((HD, QN), F32),
            buffer((2, CUT[0], QN), F32),
            buffer((KV, ROWS), BF),
            buffer((KV, ROWS), BF),
            buffer((TP, KV, 256), BF),
            buffer((2 * TP, KV, 256), BF),
            buffer((2, 2, CUT[0], ROWS), BF),
            buffer((2, 2 * TP, CUT[0], ROWS), BF),
            buffer((KV, ROWS), F32),
            dma((13,)),
            dma((2, 24)),
            dma((2, 24)),
            dma((48,)),
            dma((48,)),
            dma((10,)),
            dma((10,)),
            dma((TP,)),
            dma((TP,)),
            dma((TP,)),
            dma((TP,)),
            dma((32,)),
            dma((32,)),
        ],
        compiler_params=pltpu.CompilerParams(
            collective_id=0, has_side_effects=True, vmem_limit_bytes=52 * 1024 * 1024
        ),
    )(*[pltpu.with_memory_space_constraint(x, pltpu.HBM) for x in operands])


def shards(
    query,
    keys,
    values,
    prefix_keys,
    prefix_values,
    residual,
    out_weight,
    suffix_lens,
    req_group,
    placement,
    prefix_owner,
):
    out = whole_step(
        suffix_lens,
        req_group,
        prefix_owner,
        placement.reshape(64, 128),
        query.T,
        keys.T,
        values.T,
        prefix_keys.T,
        prefix_values.T,
        residual.T,
        out_weight,
    )
    return (out[:KV].T, out[KV : 2 * KV].T, out[2 * KV :].T)


def solution(mesh):
    return jax.shard_map(
        shards,
        mesh=mesh,
        in_specs=(
            P("seq", "tp"),
            P("seq", "tp"),
            P("seq", "tp"),
            P("seq", "tp"),
            P("seq", "tp"),
            P("seq", "tp"),
            P("tp", None),
            P(),
            P(),
            P(),
            P(),
        ),
        out_specs=(P("seq", "tp"), P("seq", "tp"), P("seq", "tp")),
        check_vma=False,
    )
```

```python
import functools
import math

import jax
import jax.numpy as jnp
from jax import lax
from jax.experimental import pallas as pl
from jax.experimental.pallas import tpu as pltpu
from jax.sharding import PartitionSpec as P

HD = 224
CUT = (128, 96)
CUT_AT = (0, 128)
ROWS = 256
PBLK = 128
PART = ROWS + PBLK
LANES = 2 * PART
QN = 2 * ROWS
KV = 2 * HD
NZ = 8
TP = 8
D = 3584
TQ = 256
NEG = -1e30
COEF = math.log2(math.e) / math.sqrt(HD)
MESH = pl.DeviceIdType.MESH
NT = (((1,), (1,)), ((), ()))
BF = jnp.bfloat16
F32 = jnp.float32


def dot(a, b):
    return jnp.dot(a, b, preferred_element_type=F32)


def dot_nt(a, b):
    return lax.dot_general(a, b, NT, preferred_element_type=F32)


def step_kernel(
    lens_hbm,
    group_hbm,
    owner_hbm,
    pos_hbm,
    q_hbm,
    k_hbm,
    v_hbm,
    pk_hbm,
    pv_hbm,
    res_hbm,
    w_hbm,
    out_ref,
    lens_ref,
    group_ref,
    owner_ref,
    pos_ref,
    res_ref,
    w_ref,
    q_own,
    q_other,
    keys,
    vals0,
    vals1,
    weights_ref,
    hot_ref,
    tops,
    q_rows,
    q_pos,
    q_start,
    q_grp,
    top,
    accum,
    cache_k,
    cache_v,
    swap_out,
    swap_in,
    w_send,
    w_all,
    att_out,
    att_all,
    projected,
    local_sem,
    ring_send,
    ring_recv,
    twin_send,
    twin_recv,
    pair_send,
    pair_recv,
    w_send_sem,
    w_recv_sem,
    w_twin_send,
    w_twin_recv,
    att_send_sem,
    att_recv_sem,
):
    hid_ref, ck_ref, cv_ref = (out_ref.at[pl.ds(i * KV, KV)] for i in range(3))
    seq = lax.axis_index("seq")
    tp = lax.axis_index("tp")
    z = seq // 4
    xh = (seq // 2) % 2
    core = seq % 2
    other = 1 - xh
    twin = 1 - core

    def dev(zz, xx, cc, tt):
        return (zz * 4 + xx * 2 + cc, tt)

    up = dev(lax.rem(z + 1, NZ), xh, core, tp)
    down = dev(lax.rem(z + NZ - 1, NZ), xh, core, tp)
    pair = dev(z, other, core, tp)
    sibling = dev(z, xh, twin, tp)

    def plane(e):
        return lax.rem(xh + e // TP, 2), lax.rem(tp + e, TP)

    mine = pl.multiple_of(xh * HD, 32)
    theirs = pl.multiple_of(other * HD, 32)
    mine_lane = pl.multiple_of(xh * PART, 128)

    blocks = (keys, vals0, vals1)
    heights = (HD,) + CUT
    offsets = (0,) + CUT_AT
    bases = (0, HD, HD + CUT[0])
    suffix = (k_hbm, v_hbm, v_hbm)
    prefix = (pk_hbm, pv_hbm, pv_hbm)

    def landing(f, lane, width):
        at = pl.multiple_of(mine_lane + lane, 128)
        return blocks[f].at[z, core, pl.ds(0, heights[f]), pl.ds(at, width)]

    def rows_of(ref, f, base):
        return ref.at[pl.ds(pl.multiple_of(base + offsets[f], 16), heights[f])]

    own = []
    for f in range(3):
        own.append(
            (
                pltpu.make_async_copy(
                    rows_of(suffix[f], f, mine), landing(f, 0, ROWS), local_sem.at[2 * f]
                ),
                pltpu.make_async_copy(
                    rows_of(prefix[f], f, mine), landing(f, ROWS, PBLK), local_sem.at[2 * f + 1]
                ),
            )
        )
    small = [
        pltpu.make_async_copy(src, dst, local_sem.at[6 + i])
        for i, (src, dst) in enumerate(
            (
                (lens_hbm, lens_ref),
                (group_hbm, group_ref),
                (owner_hbm, owner_ref),
                (pos_hbm, pos_ref),
                (q_hbm.at[pl.ds(mine, HD)], q_own),
                (w_hbm.at[pl.ds(pl.multiple_of(core * HD, 32), HD)], w_ref),
                (res_hbm, res_ref),
            )
        )
    ]
    for copy in own[0] + own[1]:
        copy.start()
    for copy in small[:5]:
        copy.start()
    for copy in own[2]:
        copy.start()
    for copy in small[5:]:
        copy.start()

    barrier = pltpu.get_barrier_semaphore()
    for peer in (up, down, sibling):
        pl.semaphore_signal(barrier, inc=1, device_id=peer, device_id_type=MESH)

    def greet(e, carry):
        xx, tt = plane(e)
        pl.semaphore_signal(barrier, inc=1, device_id=dev(z, xx, core, tt), device_id_type=MESH)
        return carry

    lax.fori_loop(1, 2 * TP, greet, 0)
    pl.semaphore_wait(barrier, 2 * TP + 2)

    def remote(src, dst, send, recv, device):
        return pltpu.make_async_remote_copy(
            src_ref=src,
            dst_ref=dst,
            send_sem=send,
            recv_sem=recv,
            device_id=device,
            device_id_type=MESH,
        )

    def pair_copy(src, dst, i):
        return remote(src, dst, pair_send.at[i], pair_recv.at[i], pair)

    exchange = [
        (
            pair_copy(rows_of(suffix[f], f, theirs), landing(f, 0, ROWS), 2 * f),
            pair_copy(rows_of(prefix[f], f, theirs), landing(f, ROWS, PBLK), 2 * f + 1),
        )
        for f in range(3)
    ]
    exchange_q = pair_copy(q_hbm.at[pl.ds(theirs, HD)], q_other, 6)

    def block(f, slot, cc, part):
        lane = pl.multiple_of(part * PART, 128)
        return blocks[f].at[slot, cc, pl.ds(0, heights[f]), pl.ds(lane, PART)]

    def ring(f, direction, slot, part, n):
        ref = block(f, slot, core, part)
        index = f * 8 + n
        return remote(
            ref,
            ref,
            ring_send.at[direction, index],
            ring_recv.at[direction, index],
            down if direction else up,
        )

    def twin_copy(f, slot, part, cc):
        ref = block(f, slot, cc, part)
        index = f * 16 + slot * 2 + part
        return remote(ref, ref, twin_send.at[index], twin_recv.at[index], sibling)

    def send_own(f, part, n):
        ring(f, 0, z, part, n).start()
        ring(f, 1, z, part, n).start()
        twin_copy(f, z, part, core).start()

    for copy in exchange[0]:
        copy.start()
    for copy in own[0]:
        copy.wait()
    send_own(0, xh, 0)
    exchange_q.start()
    for f in (1, 2):
        for copy in exchange[f]:
            copy.start()
    for copy in own[1]:
        copy.wait()
    send_own(1, xh, 0)
    for copy in own[2]:
        copy.wait()
    send_own(2, xh, 0)

    for copy in small[:5]:
        copy.wait()
    lane_ids = lax.broadcasted_iota(jnp.int32, (128, 128), 1)
    row_ids = lax.broadcasted_iota(jnp.int32, (128, 128), 0)
    for half in range(2):
        source = z * 4 + half * 2 + core
        for piece in range(2):
            row = pos_ref[pl.ds(source * 2 + piece, 1), :]
            spread = jnp.where(lane_ids == row_ids, jnp.broadcast_to(row, (128, 128)), 0)
            column = jnp.sum(spread.astype(F32), axis=1, keepdims=True)
            q_pos[pl.ds(half * ROWS + piece * 128, 128), :] = jnp.broadcast_to(
                column.astype(jnp.int32), (128, 128)
            )
    position = q_pos[...]
    start = jnp.zeros_like(position)
    group = jnp.full_like(position, group_ref[0])
    end = jnp.int32(0)
    for r in range(15):
        end = end + lens_ref[r]
        past = position >= end
        start = jnp.where(past, end, start)
        group = jnp.where(past, group_ref[r + 1], group)
    q_start[...] = start
    q_grp[...] = group
    own_q = pl.multiple_of(xh * ROWS, ROWS)
    other_q = pl.multiple_of(other * ROWS, ROWS)
    q_rows[pl.ds(own_q, ROWS), :] = jnp.transpose(q_own[...].astype(F32)).astype(BF)

    for copy in exchange[0]:
        copy.wait_recv()
    send_own(0, other, 1)
    top[...] = jnp.full_like(top, NEG)
    accum[...] = jnp.zeros_like(accum)
    cache_k[...] = jnp.zeros_like(cache_k)
    cache_v[...] = jnp.zeros_like(cache_v)
    ones = jnp.ones((16, LANES), BF)
    for slot in range(NZ):
        for cc in range(2):
            vals0[slot, cc, pl.ds(CUT[0], 16), :] = ones
    for head in range(2 * TP):
        att_all[1, head, pl.ds(CUT[1], 128 - CUT[1]), :] = jnp.zeros((128 - CUT[1], ROWS), BF)
    exchange_q.wait_recv()
    q_rows[pl.ds(other_q, ROWS), :] = jnp.transpose(q_other[...].astype(F32)).astype(BF)

    packed = lax.broadcasted_iota(jnp.int32, (ROWS, 128), 0) + (z * 4 + core) * ROWS

    def slot_at(u):
        k = (u + 1) // 2
        return lax.rem(z + jnp.where(u % 2 == 1, NZ - k, k), NZ)

    def arrived(f, slot):
        for part in range(2):
            twin_copy(f, slot, part, twin).wait_recv()

    def each_unit(f, lo, hi, body):
        def visit(i, carry):
            u = i // 2
            from_twin = i % 2
            slot = slot_at(u)

            @pl.when(from_twin == 1)
            def _():
                arrived(f, slot)

            cc = jnp.where(from_twin == 1, twin, core)
            body(slot, cc, slot * 2 + cc)
            return carry

        lax.fori_loop(lo * 2, hi * 2, visit, 0)

    def score_unit(slot, cc, unit):
        def tile(step, carry):
            rows = pl.ds(pl.multiple_of(step * TQ, TQ), TQ)
            scores = dot(q_rows[rows, :], keys[slot, cc])
            position = q_pos[rows, :]
            start = q_start[rows, :]
            group = q_grp[rows, :]
            pieces = []
            for part in range(2):
                source = slot * 4 + part * 2 + cc
                for piece in range(2):
                    at = part * PART + piece * 128
                    where = pos_ref[pl.ds(source * 2 + piece, 1), :]
                    seen = (where <= position) & (where >= start)
                    pieces.append(jnp.where(seen, scores[:, at : at + 128], NEG))
                at = part * PART + ROWS
                pieces.append(
                    jnp.where(group == owner_ref[source], scores[:, at : at + 128], NEG)
                )
            scores = jnp.concatenate(pieces, axis=1)
            fresh = jnp.maximum(top[rows, :], jnp.max(scores, axis=1, keepdims=True))
            top[rows, :] = fresh
            tops[unit, rows, :] = fresh
            weights_ref[unit, rows, :] = jnp.exp2(
                (scores - jnp.tile(fresh, (1, LANES // 128))) * COEF
            ).astype(BF)
            return carry

        lax.fori_loop(0, QN // TQ, tile, 0)

        for part in range(2):
            source = slot * 4 + part * 2 + cc
            for half in range(2):
                hot = [
                    jnp.where(
                        pos_ref[pl.ds(source * 2 + piece, 1), :] == packed + half * 2 * ROWS,
                        1.0,
                        0.0,
                    ).astype(BF)
                    for piece in range(2)
                ]
                hot_ref[unit, pl.ds(half * ROWS, ROWS), pl.ds(part * ROWS, ROWS)] = (
                    jnp.concatenate(hot, axis=1)
                )
        cache_k[...] += moved(keys, HD, slot, cc, unit)

    def moved(ref, height, slot, cc, unit):
        total = None
        for part in range(2):
            term = dot_nt(
                ref[slot, cc, pl.ds(0, height), pl.ds(part * PART, ROWS)],
                hot_ref[unit, :, pl.ds(part * ROWS, ROWS)],
            )
            total = term if total is None else total + term
        return total

    def value_unit(f, slot, cc, unit):
        ref = blocks[f]
        which = f - 1
        factor = jnp.tile(jnp.exp2((tops[unit] - top[...]) * COEF), (1, 2))
        width = ref.shape[2]
        added = dot_nt(weights_ref[unit], ref[slot, cc])
        accum[which, :, pl.ds(0, width)] = (
            accum[which, :, pl.ds(0, width)] + added * factor[:, :width]
        )
        rows = pl.ds(0, CUT[which])
        cache_v[which, rows, :] = cache_v[which, rows, :] + moved(ref, CUT[which], slot, cc, unit)

    def service(f, n):
        k = n // 2 + 1
        below = lax.rem(z + NZ - k, NZ)
        above = lax.rem(z + k, NZ)
        even = n % 2 == 0
        part = jnp.where(even, xh, other)
        part_above = jnp.where(n == 6, other, part)
        ring(f, 0, below, part, n).wait_recv()

        @pl.when(n < 5)
        def _():
            ring(f, 0, below, part, n + 2).start()

        twin_copy(f, below, part, core).start()
        ring(f, 1, above, part_above, n).wait_recv()

        @pl.when((n < 4) | (n == 5))
        def _():
            ring(f, 1, above, part, n + 2 - n // 5).start()

        twin_copy(f, above, part_above, core).start()

    def prepare_weights():
        small[5].wait()
        for t in range(TP):
            for half in range(2):
                turned = jnp.transpose(
                    w_ref[pl.ds(CUT_AT[half], CUT[half]), pl.ds(t * KV, KV)].astype(F32)
                ).astype(BF)
                if half == 1:
                    spare = jnp.zeros((KV, 128 - CUT[1]), BF)
                    turned = jnp.concatenate([turned, spare], axis=1)
                w_send[t, :, pl.ds(half * 128, 128)] = turned

        def send(e, carry):
            w_copy(e).start()
            return carry

        lax.fori_loop(1, TP, send, 0)
        w_all[2 * tp + core] = w_send[tp]
        w_twin(0, core).start()

    def w_copy(e):
        to = lax.rem(tp + e, TP)
        return remote(
            w_send.at[to],
            w_all.at[2 * tp + core],
            w_send_sem.at[e],
            w_recv_sem.at[e],
            dev(z, xh, core, to),
        )

    def w_arrival(e):
        head = 2 * lax.rem(tp + TP - e, TP) + core
        return remote(
            w_all.at[head], w_all.at[head], w_send_sem.at[e], w_recv_sem.at[e], sibling
        )

    def w_twin(e, cc):
        head = 2 * lax.rem(tp + TP - e, TP) + cc
        return remote(
            w_all.at[head], w_all.at[head], w_twin_send.at[e], w_twin_recv.at[e], sibling
        )

    def share_weights():
        def share(e, carry):
            w_arrival(e).wait_recv()
            w_twin(e, core).start()
            return carry

        lax.fori_loop(1, TP, share, 0)

    swaps = []

    def swap(i, index):
        rows = pl.ds(bases[i], heights[i])
        return pair_copy(swap_out.at[rows], swap_in.at[rows], 7 + i)

    def send_cache(i, ref):
        height, base, offset = heights[i], bases[i], offsets[i]
        out = ck_ref if i == 0 else cv_ref

        @pl.when(xh == 0)
        def _():
            swap_out[pl.ds(base, height), :] = ref[:, ROWS:].astype(BF)
            out[pl.ds(offset, height), :] = ref[:, :ROWS].astype(BF)

        @pl.when(xh == 1)
        def _():
            swap_out[pl.ds(base, height), :] = ref[:, :ROWS].astype(BF)
            out[pl.ds(HD + offset, height), :] = ref[:, ROWS:].astype(BF)

        swap(i, 0).start()

    def att_copy(half, e):
        xx, tt = plane(e)
        return remote(
            att_out.at[half, xx, pl.ds(0, CUT[half])],
            att_all.at[half, 2 * tp + xh, pl.ds(0, CUT[half])],
            att_send_sem.at[half * 16 + e],
            att_recv_sem.at[half * 16 + e],
            dev(z, xx, core, tt),
        )

    def att_head(e):
        return 2 * lax.rem(tp + 2 * TP - e, TP) + lax.rem(xh + e // TP, 2)

    def att_arrival(half, e):
        head = att_head(e)
        return remote(
            att_all.at[half, head, pl.ds(0, CUT[half])],
            att_all.at[half, head, pl.ds(0, CUT[half])],
            att_send_sem.at[half * 16 + e],
            att_recv_sem.at[half * 16 + e],
            sibling,
        )

    def finish(half):
        rows = pl.ds(0, CUT[half])
        scaled = accum[half, :, rows] / accum[0, :, pl.ds(CUT[0], 1)]
        turned = jnp.transpose(scaled).astype(BF)
        att_out[half, 0, rows, :] = turned[:, :ROWS]
        att_out[half, 1, rows, :] = turned[:, ROWS:]

        def send(e, carry):
            att_copy(half, e).start()
            return carry

        lax.fori_loop(1, 2 * TP, send, 0)
        att_all[half, 2 * tp + xh, rows, :] = att_out[half, xh, rows, :]

    def project(half):
        def add(g, carry):
            weights, rows = [], []
            for j in range(4):
                e = g * 4 + j

                @pl.when(e > 0)
                def _(e=e):
                    att_arrival(half, e).wait_recv()

                head = att_head(e)
                weights.append(w_all[head, :, pl.ds(half * 128, 128)])
                rows.append(att_all[half, head])
            projected[...] += dot(jnp.concatenate(weights, axis=1), jnp.concatenate(rows, axis=0))
            return carry

        lax.fori_loop(0, 4, add, 0)

    first_values = functools.partial(value_unit, 1)
    second_values = functools.partial(value_unit, 2)

    def round_a(i, carry):
        service(0, i)

        @pl.when(i == 1)
        def _():
            prepare_weights()

        @pl.when(i == 3)
        def _():
            for copy in exchange[1]:
                copy.wait_recv()
            send_own(1, other, 1)

        lo = jnp.where(i == 0, 0, jnp.maximum(i - 1, 1))
        each_unit(0, lo, jnp.maximum(i, 1), score_unit)
        return carry

    lax.fori_loop(0, 4, round_a, 0)

    def round_b(i, carry):
        @pl.when(i < 2)
        def _():
            service(0, i + 4)

        @pl.when(i >= 2)
        def _():
            service(1, i - 2)

        each_unit(0, i + 3, i + 4, score_unit)
        return carry

    lax.fori_loop(0, 4, round_b, 0)

    def round_c(i, carry):
        @pl.when(i == 0)
        def _():
            service(0, 6)

        @pl.when(i > 0)
        def _():
            service(1, i + 1)

        @pl.when(i == 2)
        def _():
            for copy in exchange[2]:
                copy.wait_recv()
            send_own(2, other, 1)

        @pl.when(i == 1)
        def _():
            each_unit(0, 7, 8, score_unit)

        @pl.when(i == 2)
        def _():
            send_cache(0, cache_k)
            each_unit(1, 0, 1, first_values)

        return carry

    lax.fori_loop(0, 3, round_c, 0)

    def round_d(i, carry):
        @pl.when(i < 4)
        def _():
            @pl.when(i < 2)
            def _():
                service(1, i + 4)

            @pl.when(i >= 2)
            def _():
                service(2, i - 2)

        @pl.when(i == 4)
        def _():
            service(1, 6)

        @pl.when(i > 4)
        def _():
            service(2, i - 3)

        lo = jnp.where(i < 2, 2 * i + 1, jnp.minimum(i + 3, 8))
        hi = jnp.where(i < 2, 2 * i + 3, jnp.minimum(i + 4, 8))
        each_unit(1, lo, hi, first_values)

        @pl.when(i == 2)
        def _():
            share_weights()

        @pl.when(i == 4)
        def _():
            finish(0)
            send_cache(1, cache_v.at[0, pl.ds(0, CUT[0])])

        lo = jnp.where(i == 6, 2, 0)
        hi = jnp.where(i == 6, 3, jnp.where(i == 5, 2, 0))
        each_unit(2, lo, hi, second_values)
        return carry

    lax.fori_loop(0, 7, round_d, 0)

    def round_e(i, carry):
        @pl.when(i < 2)
        def _():
            service(2, i + 4)

        @pl.when(i == 3)
        def _():
            service(2, 6)

        lo = i + 3 + i // 3
        hi = i + 4 + i // 2
        each_unit(2, lo, hi, second_values)
        return carry

    lax.fori_loop(0, 4, round_e, 0)
    finish(1)
    send_cache(2, cache_v.at[1, pl.ds(0, CUT[1])])

    for e in range(TP):
        w_twin(e, twin).wait_recv()
    small[6].wait()
    projected[...] = res_ref[...].astype(F32)
    project(0)
    for i in range(3):
        swap(i, 0).wait_recv()
    for i, out in enumerate((ck_ref, cv_ref, cv_ref)):
        height, base, offset = heights[i], bases[i], offsets[i]
        out[pl.ds(pl.multiple_of(theirs + offset, 16), height), :] = swap_in[
            pl.ds(base, height), :
        ]
    for f in range(3):
        for copy in exchange[f]:
            copy.wait_send()
        swap(f, 0).wait_send()

        def drain(n, carry, f=f):
            ring(f, 0, z, 0, n).wait_send()
            ring(f, 1, z, 0, n).wait_send()
            return carry

        lax.fori_loop(0, 7, drain, 0)

        def drain_twin(n, carry, f=f):
            twin_copy(f, n // 2, n % 2, core).wait_send()
            return carry

        lax.fori_loop(0, 16, drain_twin, 0)
    exchange_q.wait_send()

    def drain_weights(e, carry):
        @pl.when(e > 0)
        def _():
            w_copy(e).wait_send()

        w_twin(e, core).wait_send()
        return carry

    lax.fori_loop(0, TP, drain_weights, 0)

    project(1)
    hid_ref[...] = projected[...].astype(BF)

    def drain_att(e, carry):
        att_copy(0, e).wait_send()
        att_copy(1, e).wait_send()
        return carry

    lax.fori_loop(1, 2 * TP, drain_att, 0)


def whole_step(*operands):
    vmem = pl.BlockSpec(memory_space=pltpu.VMEM)
    hbm = pl.BlockSpec(memory_space=pltpu.HBM)
    shape = jax.ShapeDtypeStruct((3 * KV, ROWS), BF)
    dma = pltpu.SemaphoreType.DMA
    buffer = pltpu.VMEM
    return pl.pallas_call(
        step_kernel,
        out_shape=shape,
        in_specs=[hbm] * 11,
        out_specs=vmem,
        scratch_shapes=[
            pltpu.SMEM((16,), jnp.int32),
            pltpu.SMEM((16,), jnp.int32),
            pltpu.SMEM((32,), jnp.int32),
            buffer((64, 128), jnp.int32),
            buffer((KV, ROWS), BF),
            buffer((HD, D), BF),
            buffer((HD, ROWS), BF),
            buffer((HD, ROWS), BF),
            buffer((NZ, 2, HD, LANES), BF),
            buffer((NZ, 2, CUT[0] + 16, LANES), BF),
            buffer((NZ, 2, CUT[1], LANES), BF),
            buffer((2 * NZ, QN, LANES), BF),
            buffer((2 * NZ, QN, QN), BF),
            buffer((2 * NZ, QN, 128), F32),
            buffer((QN, HD), BF),
            buffer((QN, 128), jnp.int32),
            buffer((QN, 128), jnp.int32),
            buffer((QN, 128), jnp.int32),
            buffer((QN, 128), F32),
            buffer((2, QN, 256), F32),
            buffer((HD, QN), F32),
            buffer((2, CUT[0], QN), F32),
            buffer((KV, ROWS), BF),
            buffer((KV, ROWS), BF),
            buffer((TP, KV, 256), BF),
            buffer((2 * TP, KV, 256), BF),
            buffer((2, 2, CUT[0], ROWS), BF),
            buffer((2, 2 * TP, CUT[0], ROWS), BF),
            buffer((KV, ROWS), F32),
            dma((13,)),
            dma((2, 24)),
            dma((2, 24)),
            dma((48,)),
            dma((48,)),
            dma((10,)),
            dma((10,)),
            dma((TP,)),
            dma((TP,)),
            dma((TP,)),
            dma((TP,)),
            dma((32,)),
            dma((32,)),
        ],
        compiler_params=pltpu.CompilerParams(
            collective_id=0, has_side_effects=True, vmem_limit_bytes=52 * 1024 * 1024
        ),
    )(*[pltpu.with_memory_space_constraint(x, pltpu.HBM) for x in operands])


def shards(
    query,
    keys,
    values,
    prefix_keys,
    prefix_values,
    residual,
    out_weight,
    suffix_lens,
    req_group,
    placement,
    prefix_owner,
):
    out = whole_step(
        suffix_lens,
        req_group,
        prefix_owner,
        placement.reshape(64, 128),
        query.T,
        keys.T,
        values.T,
        prefix_keys.T,
        prefix_values.T,
        residual.T,
        out_weight,
    )
    return (out[:KV].T, out[KV : 2 * KV].T, out[2 * KV :].T)


def solution(mesh):
    return jax.shard_map(
        shards,
        mesh=mesh,
        in_specs=(
            P("seq", "tp"),
            P("seq", "tp"),
            P("seq", "tp"),
            P("seq", "tp"),
            P("seq", "tp"),
            P("seq", "tp"),
            P("tp", None),
            P(),
            P(),
            P(),
            P(),
        ),
        out_specs=(P("seq", "tp"), P("seq", "tp"), P("seq", "tp")),
        check_vma=False,
    )
```

```python
import functools
import math

import jax
import jax.numpy as jnp
from jax import lax
from jax.experimental import pallas as pl
from jax.experimental.pallas import tpu as pltpu
from jax.sharding import PartitionSpec as P

HD = 224
CUT = (128, 96)
CUT_AT = (0, 128)
ROWS = 256
PBLK = 128
PART = ROWS + PBLK
LANES = 2 * PART
QN = 2 * ROWS
KV = 2 * HD
NZ = 8
TP = 8
D = 3584
TQ = 256
NEG = -1e30
COEF = math.log2(math.e) / math.sqrt(HD)
MESH = pl.DeviceIdType.MESH
NT = (((1,), (1,)), ((), ()))
BF = jnp.bfloat16
F32 = jnp.float32


def dot(a, b):
    return jnp.dot(a, b, preferred_element_type=F32)


def dot_nt(a, b):
    return lax.dot_general(a, b, NT, preferred_element_type=F32)


def step_kernel(
    lens_hbm,
    group_hbm,
    owner_hbm,
    pos_hbm,
    q_hbm,
    k_hbm,
    v_hbm,
    pk_hbm,
    pv_hbm,
    res_hbm,
    w_hbm,
    out_ref,
    lens_ref,
    group_ref,
    owner_ref,
    pos_ref,
    res_ref,
    w_ref,
    q_own,
    q_other,
    keys,
    vals0,
    vals1,
    weights_ref,
    hot_ref,
    tops,
    q_rows,
    q_pos,
    q_start,
    q_grp,
    top,
    accum,
    cache_k,
    cache_v,
    swap_out,
    swap_in,
    w_send,
    w_all,
    att_out,
    att_all,
    projected,
    local_sem,
    ring_send,
    ring_recv,
    twin_send,
    twin_recv,
    pair_send,
    pair_recv,
    w_send_sem,
    w_recv_sem,
    w_twin_send,
    w_twin_recv,
    att_send_sem,
    att_recv_sem,
):
    hid_ref, ck_ref, cv_ref = (out_ref.at[pl.ds(i * KV, KV)] for i in range(3))
    seq = lax.axis_index("seq")
    tp = lax.axis_index("tp")
    z = seq // 4
    xh = (seq // 2) % 2
    core = seq % 2
    other = 1 - xh
    twin = 1 - core

    def dev(zz, xx, cc, tt):
        return (zz * 4 + xx * 2 + cc, tt)

    up = dev(lax.rem(z + 1, NZ), xh, core, tp)
    down = dev(lax.rem(z + NZ - 1, NZ), xh, core, tp)
    pair = dev(z, other, core, tp)
    sibling = dev(z, xh, twin, tp)

    def plane(e):
        return lax.rem(xh + e // TP, 2), lax.rem(tp + e, TP)

    mine = pl.multiple_of(xh * HD, 32)
    theirs = pl.multiple_of(other * HD, 32)
    mine_lane = pl.multiple_of(xh * PART, 128)

    blocks = (keys, vals0, vals1)
    heights = (HD,) + CUT
    offsets = (0,) + CUT_AT
    bases = (0, HD, HD + CUT[0])
    suffix = (k_hbm, v_hbm, v_hbm)
    prefix = (pk_hbm, pv_hbm, pv_hbm)

    def landing(f, lane, width):
        at = pl.multiple_of(mine_lane + lane, 128)
        return blocks[f].at[z, core, pl.ds(0, heights[f]), pl.ds(at, width)]

    def rows_of(ref, f, base):
        return ref.at[pl.ds(pl.multiple_of(base + offsets[f], 16), heights[f])]

    own = []
    for f in range(3):
        own.append(
            (
                pltpu.make_async_copy(
                    rows_of(suffix[f], f, mine), landing(f, 0, ROWS), local_sem.at[2 * f]
                ),
                pltpu.make_async_copy(
                    rows_of(prefix[f], f, mine), landing(f, ROWS, PBLK), local_sem.at[2 * f + 1]
                ),
            )
        )
    small = [
        pltpu.make_async_copy(src, dst, local_sem.at[6 + i])
        for i, (src, dst) in enumerate(
            (
                (lens_hbm, lens_ref),
                (group_hbm, group_ref),
                (owner_hbm, owner_ref),
                (pos_hbm, pos_ref),
                (q_hbm.at[pl.ds(mine, HD)], q_own),
                (w_hbm.at[pl.ds(pl.multiple_of(core * HD, 32), HD)], w_ref),
                (res_hbm, res_ref),
            )
        )
    ]
    for copy in own[0] + own[1]:
        copy.start()
    for copy in small[:5]:
        copy.start()
    for copy in own[2]:
        copy.start()
    for copy in small[5:]:
        copy.start()

    barrier = pltpu.get_barrier_semaphore()
    for peer in (up, down, sibling):
        pl.semaphore_signal(barrier, inc=1, device_id=peer, device_id_type=MESH)

    def greet(e, carry):
        xx, tt = plane(e)
        pl.semaphore_signal(barrier, inc=1, device_id=dev(z, xx, core, tt), device_id_type=MESH)
        return carry

    lax.fori_loop(1, 2 * TP, greet, 0)
    pl.semaphore_wait(barrier, 2 * TP + 2)

    def remote(src, dst, send, recv, device):
        return pltpu.make_async_remote_copy(
            src_ref=src,
            dst_ref=dst,
            send_sem=send,
            recv_sem=recv,
            device_id=device,
            device_id_type=MESH,
        )

    def pair_copy(src, dst, i):
        return remote(src, dst, pair_send.at[i], pair_recv.at[i], pair)

    exchange = [
        (
            pair_copy(rows_of(suffix[f], f, theirs), landing(f, 0, ROWS), 2 * f),
            pair_copy(rows_of(prefix[f], f, theirs), landing(f, ROWS, PBLK), 2 * f + 1),
        )
        for f in range(3)
    ]
    exchange_q = pair_copy(q_hbm.at[pl.ds(theirs, HD)], q_other, 6)

    def block(f, slot, cc, part):
        lane = pl.multiple_of(part * PART, 128)
        return blocks[f].at[slot, cc, pl.ds(0, heights[f]), pl.ds(lane, PART)]

    def ring(f, direction, slot, part, n):
        ref = block(f, slot, core, part)
        index = f * 8 + n
        return remote(
            ref,
            ref,
            ring_send.at[direction, index],
            ring_recv.at[direction, index],
            down if direction else up,
        )

    def twin_copy(f, slot, part, cc):
        ref = block(f, slot, cc, part)
        index = f * 16 + slot * 2 + part
        return remote(ref, ref, twin_send.at[index], twin_recv.at[index], sibling)

    def send_own(f, part, n):
        ring(f, 0, z, part, n).start()
        ring(f, 1, z, part, n).start()
        twin_copy(f, z, part, core).start()

    for copy in exchange[0]:
        copy.start()
    for copy in own[0]:
        copy.wait()
    send_own(0, xh, 0)
    exchange_q.start()
    for f in (1, 2):
        for copy in exchange[f]:
            copy.start()
    for copy in own[1]:
        copy.wait()
    send_own(1, xh, 0)

    for copy in small[:5]:
        copy.wait()
    lane_ids = lax.broadcasted_iota(jnp.int32, (128, 128), 1)
    row_ids = lax.broadcasted_iota(jnp.int32, (128, 128), 0)
    for half in range(2):
        source = z * 4 + half * 2 + core
        for piece in range(2):
            row = pos_ref[pl.ds(source * 2 + piece, 1), :]
            spread = jnp.where(lane_ids == row_ids, jnp.broadcast_to(row, (128, 128)), 0)
            column = jnp.sum(spread.astype(F32), axis=1, keepdims=True)
            q_pos[pl.ds(half * ROWS + piece * 128, 128), :] = jnp.broadcast_to(
                column.astype(jnp.int32), (128, 128)
            )
    position = q_pos[...]
    start = jnp.zeros_like(position)
    group = jnp.full_like(position, group_ref[0])
    end = jnp.int32(0)
    for r in range(15):
        end = end + lens_ref[r]
        past = position >= end
        start = jnp.where(past, end, start)
        group = jnp.where(past, group_ref[r + 1], group)
    q_start[...] = start
    q_grp[...] = group
    own_q = pl.multiple_of(xh * ROWS, ROWS)
    other_q = pl.multiple_of(other * ROWS, ROWS)
    q_rows[pl.ds(own_q, ROWS), :] = jnp.transpose(q_own[...].astype(F32)).astype(BF)

    top[...] = jnp.full_like(top, NEG)
    accum[...] = jnp.zeros_like(accum)
    cache_k[...] = jnp.zeros_like(cache_k)
    cache_v[...] = jnp.zeros_like(cache_v)
    ones = jnp.ones((16, LANES), BF)
    for slot in range(NZ):
        for cc in range(2):
            vals0[slot, cc, pl.ds(CUT[0], 16), :] = ones
    for head in range(2 * TP):
        att_all[1, head, pl.ds(CUT[1], 128 - CUT[1]), :] = jnp.zeros((128 - CUT[1], ROWS), BF)
    for copy in exchange[0]:
        copy.wait_recv()
    send_own(0, other, 1)
    exchange_q.wait_recv()
    q_rows[pl.ds(other_q, ROWS), :] = jnp.transpose(q_other[...].astype(F32)).astype(BF)

    packed = lax.broadcasted_iota(jnp.int32, (ROWS, 128), 0) + (z * 4 + core) * ROWS

    def slot_at(u):
        k = (u + 1) // 2
        return lax.rem(z + jnp.where(u % 2 == 1, NZ - k, k), NZ)

    def arrived(f, slot):
        for part in range(2):
            twin_copy(f, slot, part, twin).wait_recv()

    def each_unit(f, lo, hi, body):
        def visit(i, carry):
            u = i // 2
            from_twin = i % 2
            slot = slot_at(u)

            @pl.when(from_twin == 1)
            def _():
                arrived(f, slot)

            cc = jnp.where(from_twin == 1, twin, core)
            body(slot, cc, slot * 2 + cc)
            return carry

        lax.fori_loop(lo * 2, hi * 2, visit, 0)

    def score_unit(slot, cc, unit):
        def tile(step, carry):
            rows = pl.ds(pl.multiple_of(step * TQ, TQ), TQ)
            scores = dot(q_rows[rows, :], keys[slot, cc])
            position = q_pos[rows, :]
            start = q_start[rows, :]
            group = q_grp[rows, :]
            pieces = []
            for part in range(2):
                source = slot * 4 + part * 2 + cc
                for piece in range(2):
                    at = part * PART + piece * 128
                    where = pos_ref[pl.ds(source * 2 + piece, 1), :]
                    seen = (where <= position) & (where >= start)
                    pieces.append(jnp.where(seen, scores[:, at : at + 128], NEG))
                at = part * PART + ROWS
                pieces.append(
                    jnp.where(group == owner_ref[source], scores[:, at : at + 128], NEG)
                )
            scores = jnp.concatenate(pieces, axis=1)
            fresh = jnp.maximum(top[rows, :], jnp.max(scores, axis=1, keepdims=True))
            top[rows, :] = fresh
            tops[unit, rows, :] = fresh
            weights_ref[unit, rows, :] = jnp.exp2(
                (scores - jnp.tile(fresh, (1, LANES // 128))) * COEF
            ).astype(BF)
            return carry

        lax.fori_loop(0, QN // TQ, tile, 0)

        for part in range(2):
            source = slot * 4 + part * 2 + cc
            for half in range(2):
                hot = [
                    jnp.where(
                        pos_ref[pl.ds(source * 2 + piece, 1), :] == packed + half * 2 * ROWS,
                        1.0,
                        0.0,
                    ).astype(BF)
                    for piece in range(2)
                ]
                hot_ref[unit, pl.ds(half * ROWS, ROWS), pl.ds(part * ROWS, ROWS)] = (
                    jnp.concatenate(hot, axis=1)
                )
        cache_k[...] += moved(keys, HD, slot, cc, unit)

    def moved(ref, height, slot, cc, unit):
        total = None
        for part in range(2):
            term = dot_nt(
                ref[slot, cc, pl.ds(0, height), pl.ds(part * PART, ROWS)],
                hot_ref[unit, :, pl.ds(part * ROWS, ROWS)],
            )
            total = term if total is None else total + term
        return total

    def value_unit(f, slot, cc, unit):
        ref = blocks[f]
        which = f - 1
        factor = jnp.tile(jnp.exp2((tops[unit] - top[...]) * COEF), (1, 2))
        width = ref.shape[2]
        added = dot_nt(weights_ref[unit], ref[slot, cc])
        accum[which, :, pl.ds(0, width)] = (
            accum[which, :, pl.ds(0, width)] + added * factor[:, :width]
        )
        rows = pl.ds(0, CUT[which])
        cache_v[which, rows, :] = cache_v[which, rows, :] + moved(ref, CUT[which], slot, cc, unit)

    def service(f, n):
        k = n // 2 + 1
        below = lax.rem(z + NZ - k, NZ)
        above = lax.rem(z + k, NZ)
        even = n % 2 == 0
        part = jnp.where(even, xh, other)
        part_above = jnp.where(n == 6, other, part)
        ring(f, 0, below, part, n).wait_recv()

        @pl.when(n < 5)
        def _():
            ring(f, 0, below, part, n + 2).start()

        twin_copy(f, below, part, core).start()
        ring(f, 1, above, part_above, n).wait_recv()

        @pl.when((n < 4) | (n == 5))
        def _():
            ring(f, 1, above, part, n + 2 - n // 5).start()

        twin_copy(f, above, part_above, core).start()

    def prepare_weights():
        small[5].wait()
        for t in range(TP):
            for half in range(2):
                turned = jnp.transpose(
                    w_ref[pl.ds(CUT_AT[half], CUT[half]), pl.ds(t * KV, KV)].astype(F32)
                ).astype(BF)
                if half == 1:
                    spare = jnp.zeros((KV, 128 - CUT[1]), BF)
                    turned = jnp.concatenate([turned, spare], axis=1)
                w_send[t, :, pl.ds(half * 128, 128)] = turned

        def send(e, carry):
            w_copy(e).start()
            return carry

        lax.fori_loop(1, TP, send, 0)
        w_all[2 * tp + core] = w_send[tp]
        w_twin(0, core).start()

    def w_copy(e):
        to = lax.rem(tp + e, TP)
        return remote(
            w_send.at[to],
            w_all.at[2 * tp + core],
            w_send_sem.at[e],
            w_recv_sem.at[e],
            dev(z, xh, core, to),
        )

    def w_arrival(e):
        head = 2 * lax.rem(tp + TP - e, TP) + core
        return remote(
            w_all.at[head], w_all.at[head], w_send_sem.at[e], w_recv_sem.at[e], sibling
        )

    def w_twin(e, cc):
        head = 2 * lax.rem(tp + TP - e, TP) + cc
        return remote(
            w_all.at[head], w_all.at[head], w_twin_send.at[e], w_twin_recv.at[e], sibling
        )

    def share_weights():
        def share(e, carry):
            w_arrival(e).wait_recv()
            w_twin(e, core).start()
            return carry

        lax.fori_loop(1, TP, share, 0)

    swaps = []

    def swap(i, index):
        rows = pl.ds(bases[i], heights[i])
        return pair_copy(swap_out.at[rows], swap_in.at[rows], 7 + i)

    def send_cache(i, ref):
        height, base, offset = heights[i], bases[i], offsets[i]
        out = ck_ref if i == 0 else cv_ref

        @pl.when(xh == 0)
        def _():
            swap_out[pl.ds(base, height), :] = ref[:, ROWS:].astype(BF)
            out[pl.ds(offset, height), :] = ref[:, :ROWS].astype(BF)

        @pl.when(xh == 1)
        def _():
            swap_out[pl.ds(base, height), :] = ref[:, :ROWS].astype(BF)
            out[pl.ds(HD + offset, height), :] = ref[:, ROWS:].astype(BF)

        swap(i, 0).start()

    def att_copy(half, e):
        xx, tt = plane(e)
        return remote(
            att_out.at[half, xx, pl.ds(0, CUT[half])],
            att_all.at[half, 2 * tp + xh, pl.ds(0, CUT[half])],
            att_send_sem.at[half * 16 + e],
            att_recv_sem.at[half * 16 + e],
            dev(z, xx, core, tt),
        )

    def att_head(e):
        return 2 * lax.rem(tp + 2 * TP - e, TP) + lax.rem(xh + e // TP, 2)

    def att_arrival(half, e):
        head = att_head(e)
        return remote(
            att_all.at[half, head, pl.ds(0, CUT[half])],
            att_all.at[half, head, pl.ds(0, CUT[half])],
            att_send_sem.at[half * 16 + e],
            att_recv_sem.at[half * 16 + e],
            sibling,
        )

    def finish(half):
        rows = pl.ds(0, CUT[half])
        scaled = accum[half, :, rows] / accum[0, :, pl.ds(CUT[0], 1)]
        turned = jnp.transpose(scaled).astype(BF)
        att_out[half, 0, rows, :] = turned[:, :ROWS]
        att_out[half, 1, rows, :] = turned[:, ROWS:]

        def send(e, carry):
            att_copy(half, e).start()
            return carry

        lax.fori_loop(1, 2 * TP, send, 0)
        att_all[half, 2 * tp + xh, rows, :] = att_out[half, xh, rows, :]

    def project(half):
        def add(g, carry):
            weights, rows = [], []
            for j in range(4):
                e = g * 4 + j

                @pl.when(e > 0)
                def _(e=e):
                    att_arrival(half, e).wait_recv()

                head = att_head(e)
                weights.append(w_all[head, :, pl.ds(half * 128, 128)])
                rows.append(att_all[half, head])
            projected[...] += dot(jnp.concatenate(weights, axis=1), jnp.concatenate(rows, axis=0))
            return carry

        lax.fori_loop(0, 4, add, 0)

    first_values = functools.partial(value_unit, 1)
    second_values = functools.partial(value_unit, 2)

    def round_a(i, carry):
        service(0, i)

        @pl.when(i == 1)
        def _():
            prepare_weights()

        @pl.when(i == 3)
        def _():
            for copy in exchange[1]:
                copy.wait_recv()
            send_own(1, other, 1)
            for copy in own[2]:
                copy.wait()
            send_own(2, xh, 0)

        lo = jnp.where(i == 0, 0, jnp.maximum(i - 1, 1))
        each_unit(0, lo, jnp.maximum(i, 1), score_unit)
        return carry

    lax.fori_loop(0, 4, round_a, 0)

    def round_b(i, carry):
        @pl.when(i < 2)
        def _():
            service(0, i + 4)

        @pl.when(i >= 2)
        def _():
            service(1, i - 2)

        each_unit(0, i + 3, i + 4, score_unit)
        return carry

    lax.fori_loop(0, 4, round_b, 0)

    def round_c(i, carry):
        @pl.when(i == 0)
        def _():
            service(0, 6)

        @pl.when(i > 0)
        def _():
            service(1, i + 1)

        @pl.when(i == 2)
        def _():
            for copy in exchange[2]:
                copy.wait_recv()
            send_own(2, other, 1)

        @pl.when(i == 1)
        def _():
            each_unit(0, 7, 8, score_unit)

        @pl.when(i == 2)
        def _():
            send_cache(0, cache_k)
            each_unit(1, 0, 1, first_values)

        return carry

    lax.fori_loop(0, 3, round_c, 0)

    def round_d(i, carry):
        @pl.when(i < 4)
        def _():
            @pl.when(i < 2)
            def _():
                service(1, i + 4)

            @pl.when(i >= 2)
            def _():
                service(2, i - 2)

        @pl.when(i == 4)
        def _():
            service(1, 6)

        @pl.when(i > 4)
        def _():
            service(2, i - 3)

        lo = jnp.where(i < 2, 2 * i + 1, jnp.minimum(i + 3, 8))
        hi = jnp.where(i < 2, 2 * i + 3, jnp.minimum(i + 4, 8))
        each_unit(1, lo, hi, first_values)

        @pl.when(i == 2)
        def _():
            share_weights()

        @pl.when(i == 4)
        def _():
            finish(0)
            send_cache(1, cache_v.at[0, pl.ds(0, CUT[0])])

        lo = jnp.where(i == 6, 2, 0)
        hi = jnp.where(i == 6, 3, jnp.where(i == 5, 2, 0))
        each_unit(2, lo, hi, second_values)
        return carry

    lax.fori_loop(0, 7, round_d, 0)

    def round_e(i, carry):
        @pl.when(i < 2)
        def _():
            service(2, i + 4)

        @pl.when(i == 3)
        def _():
            service(2, 6)

        lo = i + 3 + i // 3
        hi = i + 4 + i // 2
        each_unit(2, lo, hi, second_values)
        return carry

    lax.fori_loop(0, 4, round_e, 0)
    finish(1)
    send_cache(2, cache_v.at[1, pl.ds(0, CUT[1])])

    for e in range(TP):
        w_twin(e, twin).wait_recv()
    small[6].wait()
    projected[...] = res_ref[...].astype(F32)
    project(0)
    for i in range(3):
        swap(i, 0).wait_recv()
    for i, out in enumerate((ck_ref, cv_ref, cv_ref)):
        height, base, offset = heights[i], bases[i], offsets[i]
        out[pl.ds(pl.multiple_of(theirs + offset, 16), height), :] = swap_in[
            pl.ds(base, height), :
        ]
    for f in range(3):
        for copy in exchange[f]:
            copy.wait_send()
        swap(f, 0).wait_send()

        def drain(n, carry, f=f):
            ring(f, 0, z, 0, n).wait_send()
            ring(f, 1, z, 0, n).wait_send()
            return carry

        lax.fori_loop(0, 7, drain, 0)

        def drain_twin(n, carry, f=f):
            twin_copy(f, n // 2, n % 2, core).wait_send()
            return carry

        lax.fori_loop(0, 16, drain_twin, 0)
    exchange_q.wait_send()

    def drain_weights(e, carry):
        @pl.when(e > 0)
        def _():
            w_copy(e).wait_send()

        w_twin(e, core).wait_send()
        return carry

    lax.fori_loop(0, TP, drain_weights, 0)

    project(1)
    hid_ref[...] = projected[...].astype(BF)

    def drain_att(e, carry):
        att_copy(0, e).wait_send()
        att_copy(1, e).wait_send()
        return carry

    lax.fori_loop(1, 2 * TP, drain_att, 0)


def whole_step(*operands):
    vmem = pl.BlockSpec(memory_space=pltpu.VMEM)
    hbm = pl.BlockSpec(memory_space=pltpu.HBM)
    shape = jax.ShapeDtypeStruct((3 * KV, ROWS), BF)
    dma = pltpu.SemaphoreType.DMA
    buffer = pltpu.VMEM
    return pl.pallas_call(
        step_kernel,
        out_shape=shape,
        in_specs=[hbm] * 11,
        out_specs=vmem,
        scratch_shapes=[
            pltpu.SMEM((16,), jnp.int32),
            pltpu.SMEM((16,), jnp.int32),
            pltpu.SMEM((32,), jnp.int32),
            buffer((64, 128), jnp.int32),
            buffer((KV, ROWS), BF),
            buffer((HD, D), BF),
            buffer((HD, ROWS), BF),
            buffer((HD, ROWS), BF),
            buffer((NZ, 2, HD, LANES), BF),
            buffer((NZ, 2, CUT[0] + 16, LANES), BF),
            buffer((NZ, 2, CUT[1], LANES), BF),
            buffer((2 * NZ, QN, LANES), BF),
            buffer((2 * NZ, QN, QN), BF),
            buffer((2 * NZ, QN, 128), F32),
            buffer((QN, HD), BF),
            buffer((QN, 128), jnp.int32),
            buffer((QN, 128), jnp.int32),
            buffer((QN, 128), jnp.int32),
            buffer((QN, 128), F32),
            buffer((2, QN, 256), F32),
            buffer((HD, QN), F32),
            buffer((2, CUT[0], QN), F32),
            buffer((KV, ROWS), BF),
            buffer((KV, ROWS), BF),
            buffer((TP, KV, 256), BF),
            buffer((2 * TP, KV, 256), BF),
            buffer((2, 2, CUT[0], ROWS), BF),
            buffer((2, 2 * TP, CUT[0], ROWS), BF),
            buffer((KV, ROWS), F32),
            dma((13,)),
            dma((2, 24)),
            dma((2, 24)),
            dma((48,)),
            dma((48,)),
            dma((10,)),
            dma((10,)),
            dma((TP,)),
            dma((TP,)),
            dma((TP,)),
            dma((TP,)),
            dma((32,)),
            dma((32,)),
        ],
        compiler_params=pltpu.CompilerParams(
            collective_id=0, has_side_effects=True, vmem_limit_bytes=52 * 1024 * 1024
        ),
    )(*[pltpu.with_memory_space_constraint(x, pltpu.HBM) for x in operands])


def shards(
    query,
    keys,
    values,
    prefix_keys,
    prefix_values,
    residual,
    out_weight,
    suffix_lens,
    req_group,
    placement,
    prefix_owner,
):
    out = whole_step(
        suffix_lens,
        req_group,
        prefix_owner,
        placement.reshape(64, 128),
        query.T,
        keys.T,
        values.T,
        prefix_keys.T,
        prefix_values.T,
        residual.T,
        out_weight,
    )
    return (out[:KV].T, out[KV : 2 * KV].T, out[2 * KV :].T)


def solution(mesh):
    return jax.shard_map(
        shards,
        mesh=mesh,
        in_specs=(
            P("seq", "tp"),
            P("seq", "tp"),
            P("seq", "tp"),
            P("seq", "tp"),
            P("seq", "tp"),
            P("seq", "tp"),
            P("tp", None),
            P(),
            P(),
            P(),
            P(),
        ),
        out_specs=(P("seq", "tp"), P("seq", "tp"), P("seq", "tp")),
        check_vma=False,
    )
```
